32 devices in a mesh: seq: 16 (over z, y, x), tp: 2 (over core).
Axes of the slice: x: 2, y: 2, z: 4, core: 2. Of those that a mesh axis runs over, the one named last changes fastest.
Arguments:
- queries: bfloat16 [8192, 4096], P('seq', 'tp'), may hold values from -9 to 9
- keys: bfloat16 [8192, 4096], P('seq', 'tp'), may hold values from -9 to 9
- values: bfloat16 [8192, 4096], P('seq', 'tp'), may hold values from -6 to 6
- route: int32 [32, 8192], P('tp', 'seq'), may hold values from 0 to 8191, as said below
- members: int32 [32, 8192], P('tp', 'seq'), may hold values from 0 to 8191, as said below
- pattern: int32 [32, 32, 10], P('tp', 'seq'), may hold values from 0 to 1, as said below
- w_out: bfloat16 [4096, 4096], P('tp', 'seq'), may hold values from -0.125 to 0.125
Outputs:
- mixed: bfloat16 [8192, 4096], P('seq', 'tp')
The draws below stay inside these ranges and needn't reach their ends.
Inputs may be any that keep to these rules, and one draw needn't show every extreme that they name: `route`: each row is a permutation of the positions; for every aligned block of 512 positions and every aligned block of 512 slots, exactly 32 of the block's positions have their slot in that slot block. members[h] is the inverse permutation of route[h]: members[h, route[h, p]] = p. `pattern`: entries 2 * 2 and 2 * 2 + 1 (the cluster's own blocks) are always 1; entries whose cluster lies outside 0 to 31 are always 0.
All inputs are finite; a program needn't handle non-finite values.
Results may differ from the reference program's by a relative error of at most 0.017.
Values may be sent and summed in bfloat16 or wider, within the bound.
No kernel may reach another device: no remote copies, remote signals or barrier semaphores. Data moves between devices by JAX's collectives and lax.ppermute only.
A program may use at most 128 MiB of HBM per device.

```python
import jax
import jax.numpy as jnp
from jax import lax

D = 4096
H = 32
HEAD = 128
CLUSTER = 256
BLOCK = 128
REACH = 2
TOK_DEV = 512
TOKENS = 8192
NCLUST = 32
N_TP = 2


def routing_tables(key):
    base_key = jax.random.fold_in(key, 7001)
    device_count = TOKENS // TOK_DEV
    per_peer = TOK_DEV // device_count

    def one_head(head_key):
        send_keys = jax.random.split(jax.random.fold_in(head_key, 1), device_count)
        land_keys = jax.random.split(jax.random.fold_in(head_key, 2), device_count)
        shuffle_send = jax.vmap(lambda inner_key: jax.random.permutation(inner_key, TOK_DEV))(send_keys).astype(jnp.int32)
        shuffle_land = jax.vmap(lambda inner_key: jax.random.permutation(inner_key, TOK_DEV))(land_keys).astype(jnp.int32)
        source = jnp.arange(device_count, dtype=jnp.int32)[:, None]
        sent_index = jnp.arange(TOK_DEV, dtype=jnp.int32)[None, :]
        target = sent_index // per_peer
        arrival = source * per_peer + sent_index % per_peer
        slots = target * TOK_DEV + shuffle_land[target, arrival]
        positions = source * TOK_DEV + shuffle_send
        route_row = jnp.zeros((TOKENS,), jnp.int32).at[positions.reshape(-1)].set(slots.reshape(-1).astype(jnp.int32))
        member_row = jnp.zeros((TOKENS,), jnp.int32).at[slots.reshape(-1)].set(positions.reshape(-1).astype(jnp.int32))
        return (route_row, member_row)
    return jax.vmap(one_head)(jax.random.split(base_key, H))


def draw_route(key, part):
    return routing_tables(key)[0]


def draw_members(key, part):
    return routing_tables(key)[1]


def draw_pattern(key, part):
    block_count = 4 * REACH + 2
    random_bits = jax.random.randint(jax.random.fold_in(key, 7002), (H, NCLUST, block_count), 0, 2).astype(jnp.int32)
    block_index = jnp.arange(block_count, dtype=jnp.int32)[None, None, :]
    cluster_index = jnp.arange(NCLUST, dtype=jnp.int32)[None, :, None]
    neighbour = cluster_index + block_index // 2 - REACH
    inside = (neighbour >= 0) & (neighbour < NCLUST)
    own_block = block_index // 2 == REACH
    return jnp.where(own_block, 1, jnp.where(inside, random_bits, 0)).astype(jnp.int32)


def attention_inputs(key):
    shape = (TOKENS, H, HEAD)
    query_key = jax.random.fold_in(key, 7003)
    other_key = jax.random.fold_in(key, 7004)
    query_base = jax.random.truncated_normal(query_key, -6.0, 6.0, shape, jnp.float32)
    key_base = jax.random.truncated_normal(other_key, -6.0, 6.0, shape, jnp.float32)
    return (query_base.reshape(TOKENS, H * HEAD), key_base.reshape(TOKENS, H * HEAD))


def draw_queries(key, part):
    return attention_inputs(key)[0].astype(jnp.bfloat16)


def draw_keys(key, part):
    return attention_inputs(key)[1].astype(jnp.bfloat16)


def strengthened(values, own_key, source, target, shards_of, factor):
    owner, partner = [(jnp.arange(values.shape[axis_at]) // (values.shape[axis_at] // shards_of)).reshape([-1 if axis == axis_at else 1 for axis in range(values.ndim)]) for axis_at in (source, target)]
    chosen = jax.random.permutation(own_key, shards_of)[partner]
    strong = (owner == chosen) | (owner == (partner + shards_of // 2) % shards_of)
    return jnp.where(strong, factor * values, values)


def level_of(own_key, shape, shards, least, high):
    level = 1.0
    for position, blocks in shards:
        draws = jax.random.uniform(jax.random.fold_in(jax.random.fold_in(own_key, 6), position), (blocks,), jnp.float32, least / len(shards), high / len(shards))
        level = level * jnp.repeat(jnp.exp(draws), shape[position] // blocks).reshape((-1,) + (1,) * (len(shape) - 1 - position))
    return level


def centred(key, dims, deviation, bound, cuts=(), kind=jnp.bfloat16):
    gain = level_of(key, dims, cuts, -0.22, 0.18) if cuts else 1.0
    entries = jax.random.normal(key, dims, jnp.float32) * deviation * gain
    return jnp.minimum(jnp.maximum(entries, -bound), bound).astype(kind)


def noise_with(key, dims, scale, most, cuts, heavy, kind=jnp.bfloat16):
    result = scale * jax.random.normal(key, dims, jnp.float32)
    if cuts:
        result = result * level_of(key, dims, cuts, -0.22, 0.18)
    return jnp.clip(strengthened(result, jax.random.fold_in(key, 3), *heavy), -most, most).astype(kind)


def setup_inputs(seed: int = 0) -> dict:
    splits = jax.random.split(jax.random.key(seed), 8)
    queries = draw_queries(jax.random.fold_in(splits[7], 71), 0)
    keys = draw_keys(jax.random.fold_in(splits[7], 71), 0)
    values = centred(splits[2], (TOKENS, H * HEAD), 1.0, 6.0, ((0, 16), (1, 2)))
    route = draw_route(jax.random.fold_in(splits[7], 71), 0)
    members = draw_members(jax.random.fold_in(splits[7], 71), 0)
    pattern = draw_pattern(jax.random.fold_in(splits[7], 71), 0)
    w_out = noise_with(splits[6], (H * HEAD, D), (H * HEAD) ** -0.5, 0.125, ((0, 2), (1, 16)), (0, 1, 16, 2.0))
    return {"queries": queries, "keys": keys, "values": values, "route": route, "members": members, "pattern": pattern, "w_out": w_out}


def window_attention(pieces):
    query_head, key_head, value_head, member_row, route_row, pattern_head = pieces
    ordered_query = jnp.take(query_head, member_row, axis=0)
    ordered_key = jnp.take(key_head, member_row, axis=0)
    ordered_value = jnp.take(value_head, member_row, axis=0)
    cluster_count = ordered_query.shape[0] // CLUSTER
    window_rows = (2 * REACH + 1) * CLUSTER
    zero_rim = jnp.zeros((REACH * CLUSTER, HEAD), ordered_key.dtype)
    padded_key = jnp.concatenate([zero_rim, ordered_key, zero_rim], axis=0)
    padded_value = jnp.concatenate([zero_rim, ordered_value, zero_rim], axis=0)
    starts = (jnp.arange(cluster_count) * CLUSTER).astype(jnp.int32)
    key_window = jax.vmap(lambda slot_start: lax.dynamic_slice_in_dim(padded_key, slot_start, window_rows, 0))(starts)
    value_window = jax.vmap(lambda slot_start: lax.dynamic_slice_in_dim(padded_value, slot_start, window_rows, 0))(starts)
    query_blocks = ordered_query.reshape(cluster_count, CLUSTER, HEAD)
    scores = jnp.einsum("cqd,ckd->cqk", query_blocks.astype(jnp.float32), key_window.astype(jnp.float32)) * (HEAD ** -0.5)
    allowed = jnp.repeat(pattern_head, BLOCK, axis=1) > 0
    scores = jnp.where(allowed[:, None, :], scores, -jnp.inf)
    row_max = jnp.max(scores, axis=-1, keepdims=True)
    exponent = jnp.exp(scores - row_max)
    weights = (exponent / jnp.sum(exponent, axis=-1, keepdims=True)).astype(jnp.bfloat16)
    context = jnp.einsum("cqk,ckd->cqd", weights.astype(jnp.float32), value_window.astype(jnp.float32)).astype(jnp.bfloat16)
    context = context.reshape(cluster_count * CLUSTER, HEAD)
    return jnp.take(context, route_row, axis=0)


def reference(queries, keys, values, route, members, pattern, w_out):
    token_count = queries.shape[0]

    def by_head(input_array):
        return input_array.reshape(token_count, H, HEAD).transpose(1, 0, 2)

    context = lax.map(window_attention, (by_head(queries), by_head(keys), by_head(values), members, route, pattern))
    attended = context.transpose(1, 0, 2).reshape(token_count, H * HEAD)
    group_width = (H // N_TP) * HEAD
    summed = jnp.zeros((token_count, D), jnp.float32)
    for group_index in range(N_TP):
        lower_edge = group_index * group_width
        partial_value = jnp.dot(attended[:, lower_edge:lower_edge + group_width], w_out[lower_edge:lower_edge + group_width], preferred_element_type=jnp.float32)
        rounded = lax.optimization_barrier(partial_value.astype(jnp.bfloat16))
        summed = summed + rounded.astype(jnp.float32)
    return summed.astype(jnp.bfloat16)
```

```python
import jax
import jax.numpy as jnp
from jax import lax
from jax.experimental import pallas as pl
from jax.experimental.pallas import tpu as pltpu
from jax.sharding import PartitionSpec as P

CLUSTER = 256
REACH = 2


def extended_2(cells, sides, width):
    for axis, dim in sides:
        count = lax.axis_size(axis)
        ends = count - 1
        head = lax.slice_in_dim(cells, 0, width, axis=dim)
        tail = lax.slice_in_dim(cells, cells.shape[dim] - width, cells.shape[dim], axis=dim)
        cells = jnp.concatenate(
            [
                lax.ppermute(tail, axis, [(i, (i + 1) % count) for i in range(ends)]),
                cells,
                lax.ppermute(head, axis, [((i + 1) % count, i) for i in range(ends)]),
            ],
            axis=dim,
        )
    return cells


def attend_head(pieces):
    query_rows, key_rows, value_rows, pattern_rows = pieces
    head_width = query_rows.shape[1]
    cluster_count = query_rows.shape[0] // CLUSTER
    window_rows = (2 * REACH + 1) * CLUSTER
    starts = jnp.arange(cluster_count) * CLUSTER
    key_window = jax.vmap(
        lambda slot_start: lax.dynamic_slice_in_dim(key_rows, slot_start, window_rows, 0)
    )(starts)
    value_window = jax.vmap(
        lambda slot_start: lax.dynamic_slice_in_dim(value_rows, slot_start, window_rows, 0)
    )(starts)
    query_blocks = query_rows.reshape(cluster_count, CLUSTER, head_width)
    scores = jnp.einsum(
        "cqd,ckd->cqk", query_blocks, key_window, preferred_element_type=jnp.float32
    ) * head_width ** (-0.5)
    allowed = jnp.repeat(pattern_rows, CLUSTER // 2, axis=1) > 0
    scores = jnp.where(allowed[:, None, :], scores, -jnp.inf)
    row_max = jnp.max(scores, axis=-1, keepdims=True)
    exponent = jnp.exp(scores - row_max)
    weights = (exponent / jnp.sum(exponent, axis=-1, keepdims=True)).astype(jnp.bfloat16)
    context = jnp.einsum(
        "cqk,ckd->cqd", weights, value_window, preferred_element_type=jnp.float32
    ).astype(jnp.bfloat16)
    return context.reshape(query_rows.shape[0], head_width)


def buffer_index(group_of, order_key, per_peer):
    same_group = group_of[:, :, None] == group_of[:, None, :]
    earlier = order_key[:, None, :] < order_key[:, :, None]
    rank = jnp.sum((same_group & earlier).astype(jnp.int32), axis=2)
    return group_of * per_peer + rank


def slot_shards(queries, keys, values, route, members, pattern, w_out):
    rows_here = queries.shape[0]
    head_count = route.shape[0]
    head_width = queries.shape[1] // head_count
    peer_count = lax.axis_size("seq")
    per_peer = rows_here // peer_count
    local_iota = jnp.arange(rows_here, dtype=jnp.int32)
    send_index = buffer_index(route // rows_here, route, per_peer)
    local_slots = jnp.broadcast_to(local_iota[None, :], members.shape)
    arrival_index = buffer_index(members // rows_here, local_slots, per_peer)
    send_table = (send_index[:, None, :] == local_iota[None, :, None]).astype(jnp.bfloat16)
    land_table = (arrival_index[:, :, None] == local_iota[None, None, :]).astype(jnp.bfloat16)
    stacked = jnp.concatenate(
        [
            queries.reshape(rows_here, head_count, head_width),
            keys.reshape(rows_here, head_count, head_width),
            values.reshape(rows_here, head_count, head_width),
        ],
        axis=2,
    )
    packed = jnp.einsum(
        "hap,phd->had", send_table, stacked, preferred_element_type=jnp.float32
    ).astype(jnp.bfloat16)

    def outgoing(column_index):
        part_rows = packed[:, :, column_index * head_width : (column_index + 1) * head_width]
        return part_rows.reshape(head_count, peer_count, per_peer, head_width)

    sent_query, sent_key, sent_value = (
        lax.all_to_all(outgoing(0), "seq", split_axis=1, concat_axis=1, tiled=True),
        lax.all_to_all(outgoing(1), "seq", split_axis=1, concat_axis=1, tiled=True),
        lax.all_to_all(outgoing(2), "seq", split_axis=1, concat_axis=1, tiled=True),
    )
    arrived = jnp.concatenate(
        [
            sent_query.reshape(head_count, rows_here, head_width),
            sent_key.reshape(head_count, rows_here, head_width),
            sent_value.reshape(head_count, rows_here, head_width),
        ],
        axis=2,
    )
    placed = jnp.einsum(
        "hsa,had->hsd", land_table, arrived, preferred_element_type=jnp.float32
    ).astype(jnp.bfloat16)
    ordered_query = placed[:, :, :head_width]
    keys_values = jnp.stack(
        [placed[:, :, head_width : 2 * head_width], placed[:, :, 2 * head_width :]]
    )
    extended = extended_2(keys_values, (("seq", 2),), REACH * CLUSTER)
    context = lax.map(attend_head, (ordered_query, extended[0], extended[1], pattern))
    returning = jnp.einsum(
        "hsa,hsd->had", land_table, context, preferred_element_type=jnp.float32
    ).astype(jnp.bfloat16)
    returning = returning.reshape(head_count, peer_count, per_peer, head_width)
    returned = lax.all_to_all(returning, "seq", split_axis=1, concat_axis=1, tiled=True).reshape(
        head_count, rows_here, head_width
    )
    attended = jnp.einsum(
        "hap,had->phd", send_table, returned, preferred_element_type=jnp.float32
    ).astype(jnp.bfloat16)
    attended = attended.reshape(rows_here, head_count * head_width)
    partial_value = jnp.dot(
        attended,
        lax.all_gather(w_out, "seq", axis=1, tiled=True),
        preferred_element_type=jnp.float32,
    )
    mixed_out = lax.psum_scatter(
        partial_value.astype(jnp.bfloat16), "tp", scatter_dimension=1, tiled=True
    )
    return mixed_out


LANES = 128
BLOCK = 128


def order_of(key_row):
    n = key_row.shape[1]
    key_col = jnp.broadcast_to(key_row, (LANES, n)).T
    counts = []
    for j in range(n // LANES):
        less = key_col < key_row[:, j * LANES : (j + 1) * LANES]
        counts.append(jnp.sum(jnp.where(less, 1, 0), axis=0, keepdims=True))
    return jnp.concatenate(counts, axis=1)


def table_to(order_row):
    n = order_row.shape[1]
    rows = lax.broadcasted_iota(jnp.int32, (n, n), 0)
    return jnp.where(rows == order_row, 1.0, 0.0).astype(jnp.bfloat16)


def table_from(order_row):
    n = order_row.shape[1]
    order_col = jnp.broadcast_to(order_row, (LANES, n)).T
    lane = lax.broadcasted_iota(jnp.int32, (n, LANES), 1)
    parts = [
        jnp.where(order_col == lane + j * LANES, 1.0, 0.0).astype(jnp.bfloat16)
        for j in range(n // LANES)
    ]
    return jnp.concatenate(parts, axis=1)


def mm(a, b):
    return jnp.dot(a, b, preferred_element_type=jnp.float32)


def pack(route, queries, keys, values):
    heads, rows = route.shape
    width = queries.shape[1] // heads

    def kernel(route_ref, q_ref, k_ref, v_ref, out_ref, order_ref):
        h = pl.program_id(0)
        order = order_of(route_ref[pl.ds(h, 1), :])
        order_ref[0] = order
        table = table_to(order)
        out_ref[0, 0] = mm(table, q_ref[...]).astype(jnp.bfloat16)
        out_ref[0, 1] = mm(table, k_ref[...]).astype(jnp.bfloat16)
        out_ref[0, 2] = mm(table, v_ref[...]).astype(jnp.bfloat16)

    columns = pl.BlockSpec((rows, width), lambda h: (0, h))
    return pl.pallas_call(
        kernel,
        name="pack",
        grid=(heads,),
        in_specs=[pl.BlockSpec((heads, rows), lambda h: (0, 0)), columns, columns, columns],
        out_specs=[
            pl.BlockSpec((1, 3, rows, width), lambda h: (h, 0, 0, 0)),
            pl.BlockSpec((1, 1, rows), lambda h: (h, 0, 0)),
        ],
        out_shape=[
            jax.ShapeDtypeStruct((heads, 3, rows, width), jnp.bfloat16),
            jax.ShapeDtypeStruct((heads, 1, rows), jnp.int32),
        ],
    )(route, queries, keys, values)


def attend(members, pattern, arrived):
    nb, rows = members.shape
    senders, _, _, width = arrived.shape
    per = rows // senders
    per_block = rows // CLUSTER
    window = (2 * REACH + 1) * CLUSTER
    blocks = window // BLOCK
    margin = REACH * CLUSTER
    lag = margin // rows
    total = nb * rows + 2 * margin
    scale = width ** (-0.5) * 1.4426950408889634

    def kernel(pat_ref, mem_ref, in_ref, out_ref, kbuf, vbuf, qbuf, arr):
        g = pl.program_id(0)

        @pl.when(g == 0)
        def _():
            zero = jnp.zeros((margin, width), jnp.bfloat16)
            for at in (0, total - margin):
                kbuf[at : at + margin, :] = zero
                vbuf[at : at + margin, :width] = zero
            vbuf[:, width:] = jnp.ones((total, width), jnp.bfloat16)

        @pl.when(g < nb)
        def _():
            row = mem_ref[pl.ds(g, 1), :]
            slot = lax.broadcasted_iota(jnp.int32, (1, rows), 1)
            order = order_of(jnp.bitwise_or(jnp.bitwise_and(row, -rows), slot))
            arr[pl.ds(g % 2, 1)] = order[None]
            table = table_from(order)
            at = pl.multiple_of(g * rows + margin, rows)
            put = [
                mm(table, in_ref[:, i].reshape(rows, width)).astype(jnp.bfloat16)
                for i in range(3)
            ]
            qbuf[pl.ds(g % 2, 1)] = put[0][None]
            kbuf[pl.ds(at, rows), :] = put[1]
            vbuf[pl.ds(at, rows), :width] = put[2]

        @pl.when(g >= lag)
        def _():
            b = g - lag
            contexts = []
            for i in range(per_block):
                q = qbuf[pl.ds(b % 2, 1), i * CLUSTER : (i + 1) * CLUSTER, :][0]
                at = pl.multiple_of(b * rows + i * CLUSTER, CLUSTER)
                scores = lax.dot_general(
                    q,
                    kbuf[pl.ds(at, window), :],
                    (((1,), (1,)), ((), ())),
                    preferred_element_type=jnp.float32,
                )
                parts = []
                for j in range(blocks):
                    allowed = pat_ref[(b * per_block + i) * blocks + j] > 0
                    shift = jnp.where(allowed, 0.0, -jnp.inf)
                    parts.append(scores[:, j * BLOCK : (j + 1) * BLOCK] + shift)
                most = parts[0]
                for part in parts[1:]:
                    most = jnp.maximum(most, part)
                most = jnp.max(most, axis=1, keepdims=True)
                weights = jnp.concatenate(
                    [jnp.exp2((part - most) * scale).astype(jnp.bfloat16) for part in parts], axis=1
                )
                both = mm(weights, vbuf[pl.ds(at, window), :])
                contexts.append((both[:, :width] / both[:, width:]).astype(jnp.bfloat16))
            context = jnp.concatenate(contexts, axis=0)
            back = mm(table_to(arr[pl.ds(b % 2, 1)][0]), context).astype(jnp.bfloat16)
            out_ref[...] = back.reshape(senders, per, width)

    return pl.pallas_call(
        kernel,
        name="attend",
        grid_spec=pltpu.PrefetchScalarGridSpec(
            num_scalar_prefetch=1,
            grid=(nb + lag,),
            in_specs=[
                pl.BlockSpec((nb, rows), lambda g, p: (0, 0)),
                pl.BlockSpec((senders, 3, per, width), lambda g, p: (0, 0, jnp.minimum(g, nb - 1), 0)),
            ],
            out_specs=pl.BlockSpec((senders, per, width), lambda g, p: (0, jnp.maximum(g - lag, 0), 0)),
            scratch_shapes=[
                pltpu.VMEM((total, width), jnp.bfloat16),
                pltpu.VMEM((total, 2 * width), jnp.bfloat16),
                pltpu.VMEM((2, rows, width), jnp.bfloat16),
                pltpu.VMEM((2, 1, rows), jnp.int32),
            ],
        ),
        out_shape=jax.ShapeDtypeStruct((senders, nb * per, width), jnp.bfloat16),
    )(pattern, members, arrived)


def unpack(order, returned):
    heads, rows, width = returned.shape

    def kernel(order_ref, in_ref, out_ref):
        out_ref[...] = mm(table_from(order_ref[0]), in_ref[0]).astype(jnp.bfloat16)

    return pl.pallas_call(
        kernel,
        name="unpack",
        grid=(heads,),
        in_specs=[
            pl.BlockSpec((1, 1, rows), lambda h: (h, 0, 0)),
            pl.BlockSpec((1, rows, width), lambda h: (h, 0, 0)),
        ],
        out_specs=pl.BlockSpec((rows, width), lambda h: (0, h)),
        out_shape=jax.ShapeDtypeStruct((rows, heads * width), jnp.bfloat16),
    )(order, returned)


def project(pieces, pieces_too, attended, first, second):
    count = pieces.shape[0]
    rows, depth = attended.shape
    half, cols = first.shape[1:]

    def kernel(at_ref, too_ref, a_ref, f_ref, s_ref, out_ref):
        out_ref[...] = (mm(a_ref[:, :half], f_ref[0]) + mm(a_ref[:, half:], s_ref[0])).astype(
            jnp.bfloat16
        )

    return pl.pallas_call(
        kernel,
        name="project",
        grid_spec=pltpu.PrefetchScalarGridSpec(
            num_scalar_prefetch=2,
            grid=(count,),
            in_specs=[
                pl.BlockSpec((rows, depth), lambda j, at, too: (0, 0)),
                pl.BlockSpec((1, half, cols), lambda j, at, too: (at[j], 0, 0)),
                pl.BlockSpec((1, half, cols), lambda j, at, too: (too[j], 0, 0)),
            ],
            out_specs=pl.BlockSpec((rows, cols), lambda j, at, too: (0, j)),
        ),
        out_shape=jax.ShapeDtypeStruct((rows, count * cols), jnp.bfloat16),
    )(pieces, pieces_too, attended, first, second)


def gather_weights(w_out):
    count = lax.axis_size("seq")
    line = count // 4
    me = lax.axis_index("seq")
    right = [(i, i + 4) for i in range(count - 4)]
    left = [(i + 4, i) for i in range(count - 4)]
    from_left, from_right = [w_out], [w_out]
    for _ in range(line - 1):
        from_left.append(lax.ppermute(from_left[-1], "seq", right))
        from_right.append(lax.ppermute(from_right[-1], "seq", left))
    stack = [w_out] + [from_left[k] + from_right[line - k] for k in range(1, line)]
    half = w_out.shape[0] // 2

    def doubled(cells, bit):
        other = lax.ppermute(cells, "seq", [(i, i ^ bit) for i in range(count)])
        return jnp.concatenate([cells, other], axis=0)

    first = doubled(doubled(jnp.stack([cell[:half] for cell in stack]), 2), 1)
    second = doubled(doubled(jnp.stack([cell[half:] for cell in stack]), 1), 2)
    names = jnp.arange(count, dtype=jnp.int32)
    step = jnp.mod(me // 4 - names // 4, line)
    differ = jnp.bitwise_xor(me, names)
    low, high = differ % 2, (differ // 2) % 2
    return first, second, (low * 2 + high) * line + step, (high * 2 + low) * line + step


def head_shards(queries, keys, values, route, members, pattern, w_out):
    heads, rows = route.shape
    count = lax.axis_size("seq")
    extra = pattern.shape[1] * pattern.shape[2]
    meta = jnp.concatenate(
        [
            members,
            pattern.reshape(heads, extra),
            jnp.zeros((heads, LANES - extra), jnp.int32),
        ],
        axis=1,
    )
    meta = lax.all_to_all(meta, "seq", split_axis=0, concat_axis=0, tiled=True)
    packed, order = pack(route, queries, keys, values)
    arrived = lax.all_to_all(packed, "seq", split_axis=0, concat_axis=0, tiled=True)
    first, second, at_first, at_second = gather_weights(w_out)
    context = attend(meta[:, :rows], meta[:, rows : rows + extra].reshape(-1), arrived)
    returned = lax.all_to_all(context, "seq", split_axis=0, concat_axis=0, tiled=True)
    attended = unpack(order, returned)
    mine = lax.axis_index("tp")
    half = count // 2

    def part(which):
        places = [lax.dynamic_slice_in_dim(at, which * half, half) for at in (at_first, at_second)]
        return project(places[0], places[1], attended, first, second)

    send = part(1 - mine)
    received = lax.ppermute(send, "tp", [(0, 1), (1, 0)])
    keep = part(mine)
    return (keep.astype(jnp.float32) + received.astype(jnp.float32)).astype(jnp.bfloat16)


def choose(mesh):
    count, groups = mesh.shape["seq"], mesh.shape["tp"]

    def shards(queries, keys, values, route, members, pattern, w_out):
        heads, rows = route.shape
        split = heads == count and groups == 2 and count % 4 == 0
        tiles = rows == REACH * CLUSTER and queries.shape[1] == heads * LANES
        body = head_shards if split and tiles else slot_shards
        return body(queries, keys, values, route, members, pattern, w_out)

    return shards


def solution(mesh):
    placed = (
        P("seq", "tp"),
        P("seq", "tp"),
        P("seq", "tp"),
        P("tp", "seq"),
        P("tp", "seq"),
        P("tp", "seq", None),
        P("tp", "seq"),
    )
    return jax.shard_map(
        choose(mesh), mesh=mesh, in_specs=placed, out_specs=P("seq", "tp"), check_vma=False
    )
```

```python
import jax
import jax.numpy as jnp
from jax import lax
from jax.experimental import pallas as pl
from jax.experimental.pallas import tpu as pltpu
from jax.sharding import PartitionSpec as P


CLUSTER = 256
REACH = 2


def extended_2(cells, sides, width):
    for axis, dim in sides:
        count = lax.axis_size(axis)
        ends = count - 1
        head = lax.slice_in_dim(cells, 0, width, axis=dim)
        tail = lax.slice_in_dim(cells, cells.shape[dim] - width, cells.shape[dim], axis=dim)
        cells = jnp.concatenate(
            [
                lax.ppermute(tail, axis, [(i, (i + 1) % count) for i in range(ends)]),
                cells,
                lax.ppermute(head, axis, [((i + 1) % count, i) for i in range(ends)]),
            ],
            axis=dim,
        )
    return cells


def attend_head(pieces):
    query_rows, key_rows, value_rows, pattern_rows = pieces
    head_width = query_rows.shape[1]
    cluster_count = query_rows.shape[0] // CLUSTER
    window_rows = (2 * REACH + 1) * CLUSTER
    starts = jnp.arange(cluster_count) * CLUSTER
    key_window = jax.vmap(
        lambda slot_start: lax.dynamic_slice_in_dim(key_rows, slot_start, window_rows, 0)
    )(starts)
    value_window = jax.vmap(
        lambda slot_start: lax.dynamic_slice_in_dim(value_rows, slot_start, window_rows, 0)
    )(starts)
    query_blocks = query_rows.reshape(cluster_count, CLUSTER, head_width)
    scores = jnp.einsum(
        "cqd,ckd->cqk", query_blocks, key_window, preferred_element_type=jnp.float32
    ) * head_width ** (-0.5)
    allowed = jnp.repeat(pattern_rows, CLUSTER // 2, axis=1) > 0
    scores = jnp.where(allowed[:, None, :], scores, -jnp.inf)
    row_max = jnp.max(scores, axis=-1, keepdims=True)
    exponent = jnp.exp(scores - row_max)
    weights = (exponent / jnp.sum(exponent, axis=-1, keepdims=True)).astype(jnp.bfloat16)
    context = jnp.einsum(
        "cqk,ckd->cqd", weights, value_window, preferred_element_type=jnp.float32
    ).astype(jnp.bfloat16)
    return context.reshape(query_rows.shape[0], head_width)


def buffer_index(group_of, order_key, per_peer):
    same_group = group_of[:, :, None] == group_of[:, None, :]
    earlier = order_key[:, None, :] < order_key[:, :, None]
    rank = jnp.sum((same_group & earlier).astype(jnp.int32), axis=2)
    return group_of * per_peer + rank


def slot_shards(queries, keys, values, route, members, pattern, w_out):
    rows_here = queries.shape[0]
    head_count = route.shape[0]
    head_width = queries.shape[1] // head_count
    peer_count = lax.axis_size("seq")
    per_peer = rows_here // peer_count
    local_iota = jnp.arange(rows_here, dtype=jnp.int32)
    send_index = buffer_index(route // rows_here, route, per_peer)
    local_slots = jnp.broadcast_to(local_iota[None, :], members.shape)
    arrival_index = buffer_index(members // rows_here, local_slots, per_peer)
    send_table = (send_index[:, None, :] == local_iota[None, :, None]).astype(jnp.bfloat16)
    land_table = (arrival_index[:, :, None] == local_iota[None, None, :]).astype(jnp.bfloat16)
    stacked = jnp.concatenate(
        [
            queries.reshape(rows_here, head_count, head_width),
            keys.reshape(rows_here, head_count, head_width),
            values.reshape(rows_here, head_count, head_width),
        ],
        axis=2,
    )
    packed = jnp.einsum(
        "hap,phd->had", send_table, stacked, preferred_element_type=jnp.float32
    ).astype(jnp.bfloat16)

    def outgoing(column_index):
        part_rows = packed[:, :, column_index * head_width : (column_index + 1) * head_width]
        return part_rows.reshape(head_count, peer_count, per_peer, head_width)

    sent_query, sent_key, sent_value = (
        lax.all_to_all(outgoing(0), "seq", split_axis=1, concat_axis=1, tiled=True),
        lax.all_to_all(outgoing(1), "seq", split_axis=1, concat_axis=1, tiled=True),
        lax.all_to_all(outgoing(2), "seq", split_axis=1, concat_axis=1, tiled=True),
    )
    arrived = jnp.concatenate(
        [
            sent_query.reshape(head_count, rows_here, head_width),
            sent_key.reshape(head_count, rows_here, head_width),
            sent_value.reshape(head_count, rows_here, head_width),
        ],
        axis=2,
    )
    placed = jnp.einsum(
        "hsa,had->hsd", land_table, arrived, preferred_element_type=jnp.float32
    ).astype(jnp.bfloat16)
    ordered_query = placed[:, :, :head_width]
    keys_values = jnp.stack(
        [placed[:, :, head_width : 2 * head_width], placed[:, :, 2 * head_width :]]
    )
    extended = extended_2(keys_values, (("seq", 2),), REACH * CLUSTER)
    context = lax.map(attend_head, (ordered_query, extended[0], extended[1], pattern))
    returning = jnp.einsum(
        "hsa,hsd->had", land_table, context, preferred_element_type=jnp.float32
    ).astype(jnp.bfloat16)
    returning = returning.reshape(head_count, peer_count, per_peer, head_width)
    returned = lax.all_to_all(returning, "seq", split_axis=1, concat_axis=1, tiled=True).reshape(
        head_count, rows_here, head_width
    )
    attended = jnp.einsum(
        "hap,had->phd", send_table, returned, preferred_element_type=jnp.float32
    ).astype(jnp.bfloat16)
    attended = attended.reshape(rows_here, head_count * head_width)
    partial_value = jnp.dot(
        attended,
        lax.all_gather(w_out, "seq", axis=1, tiled=True),
        preferred_element_type=jnp.float32,
    )
    mixed_out = lax.psum_scatter(
        partial_value.astype(jnp.bfloat16), "tp", scatter_dimension=1, tiled=True
    )
    return mixed_out


LANES = 128
DIGIT = 4
TAIL = 32
BLOCK = 128


def order_of(key_row):
    n = key_row.shape[1]
    key_col = jnp.broadcast_to(key_row, (LANES, n)).T
    counts = []
    for j in range(n // LANES):
        less = key_col < key_row[:, j * LANES : (j + 1) * LANES]
        counts.append(jnp.sum(jnp.where(less, 1, 0), axis=0, keepdims=True))
    return jnp.concatenate(counts, axis=1)


def table_to(order_row):
    n = order_row.shape[1]
    rows = lax.broadcasted_iota(jnp.int32, (n, n), 0)
    return jnp.where(rows == order_row, 1.0, 0.0).astype(jnp.bfloat16)


def table_from(order_row):
    n = order_row.shape[1]
    order_col = jnp.broadcast_to(order_row, (LANES, n)).T
    lane = lax.broadcasted_iota(jnp.int32, (n, LANES), 1)
    parts = [
        jnp.where(order_col == lane + j * LANES, 1.0, 0.0).astype(jnp.bfloat16)
        for j in range(n // LANES)
    ]
    return jnp.concatenate(parts, axis=1)


def mm(a, b):
    return jnp.dot(a, b, preferred_element_type=jnp.float32)


def pack(route, pattern, queries, keys, values):
    heads, rows = route.shape
    width = queries.shape[1] // heads
    lines = rows // LANES

    def kernel(route_ref, pat_ref, q_ref, k_ref, v_ref, out_ref, order_ref):
        h = pl.program_id(0)
        row = route_ref[pl.ds(h, 1), :]
        order = order_of(row)
        order_ref[0] = order
        table = table_to(order)
        out_ref[0, 0:rows] = mm(table, q_ref[...]).astype(jnp.bfloat16)
        out_ref[0, rows : 2 * rows] = mm(table, k_ref[...]).astype(jnp.bfloat16)
        out_ref[0, 2 * rows : 3 * rows] = mm(table, v_ref[...]).astype(jnp.bfloat16)
        slot = jnp.bitwise_and(row, rows - 1)
        high = lax.shift_right_logical(slot, DIGIT)
        low = jnp.bitwise_and(slot, (1 << DIGIT) - 1)
        at = lax.broadcasted_iota(jnp.int32, (8, rows), 0)
        digits = jnp.where(at == 0, high, jnp.where(at == 1, low, 0))
        digits = digits.astype(jnp.float32).astype(jnp.bfloat16)
        sorted_digits = lax.dot_general(
            digits, table, (((1,), (1,)), ((), ())), preferred_element_type=jnp.float32
        )
        parts = [
            sorted_digits[d : d + 1, j * LANES : (j + 1) * LANES] for d in range(2) for j in range(lines)
        ]
        parts.append(pat_ref[pl.ds(h, 1), :].astype(jnp.float32))
        parts.append(jnp.zeros((TAIL - 2 * lines - 1, LANES), jnp.float32))
        out_ref[0, 3 * rows :] = jnp.concatenate(parts, axis=0).astype(jnp.bfloat16)

    columns = pl.BlockSpec((rows, width), lambda h: (0, h))
    total = 3 * rows + TAIL
    return pl.pallas_call(
        kernel,
        name="pack",
        grid=(heads,),
        in_specs=[
            pl.BlockSpec((heads, rows), lambda h: (0, 0)),
            pl.BlockSpec((heads, LANES), lambda h: (0, 0)),
            columns,
            columns,
            columns,
        ],
        out_specs=[
            pl.BlockSpec((1, total, width), lambda h: (h, 0, 0)),
            pl.BlockSpec((1, 1, rows), lambda h: (h, 0, 0)),
        ],
        out_shape=[
            jax.ShapeDtypeStruct((heads, total, width), jnp.bfloat16),
            jax.ShapeDtypeStruct((heads, 1, rows), jnp.int32),
        ],
    )(route, pattern, queries, keys, values)


def tail_of(arrived, rows, entries):
    senders = arrived.shape[0]
    lines = rows // LANES
    tail = arrived[:, 3 * rows : 3 * rows + 2 * lines + 1].astype(jnp.int32)
    slot = (tail[:, :lines] << DIGIT) + tail[:, lines : 2 * lines]
    slot = slot.reshape(senders, senders, rows // senders).transpose(1, 0, 2)
    return slot.reshape(senders, rows), tail[:, 2 * lines, :entries].reshape(-1)


def attend(slots, pattern, arrived):
    nb, rows = slots.shape
    senders, _, width = arrived.shape
    per = rows // senders
    per_block = rows // CLUSTER
    window = (2 * REACH + 1) * CLUSTER
    blocks = window // BLOCK
    margin = REACH * CLUSTER
    lag = margin // rows
    total = nb * rows + 2 * margin
    scale = width ** (-0.5) * 1.4426950408889634

    def kernel(pat_ref, slot_ref, q_ref, k_ref, v_ref, out_ref, kbuf, vbuf, qbuf):
        g = pl.program_id(0)

        @pl.when(g == 0)
        def _():
            zero = jnp.zeros((margin, width), jnp.bfloat16)
            for at in (0, total - margin):
                kbuf[at : at + margin, :] = zero
                vbuf[at : at + margin, :width] = zero
            vbuf[:, width:] = jnp.ones((total, width), jnp.bfloat16)

        @pl.when(g < nb)
        def _():
            table = table_to(slot_ref[pl.ds(g, 1), :])
            at = pl.multiple_of(g * rows + margin, rows)
            put = [
                mm(table, ref[...].reshape(rows, width)).astype(jnp.bfloat16)
                for ref in (q_ref, k_ref, v_ref)
            ]
            qbuf[pl.ds(g % 2, 1)] = put[0][None]
            kbuf[pl.ds(at, rows), :] = put[1]
            vbuf[pl.ds(at, rows), :width] = put[2]

        @pl.when(g >= lag)
        def _():
            b = g - lag
            contexts = []
            for i in range(per_block):
                q = qbuf[pl.ds(b % 2, 1), i * CLUSTER : (i + 1) * CLUSTER, :][0]
                at = pl.multiple_of(b * rows + i * CLUSTER, CLUSTER)
                scores = lax.dot_general(
                    q,
                    kbuf[pl.ds(at, window), :],
                    (((1,), (1,)), ((), ())),
                    preferred_element_type=jnp.float32,
                )
                parts = []
                for j in range(blocks):
                    allowed = pat_ref[(b * per_block + i) * blocks + j] > 0
                    shift = jnp.where(allowed, 0.0, -jnp.inf)
                    parts.append(scores[:, j * BLOCK : (j + 1) * BLOCK] + shift)
                most = parts[0]
                for part in parts[1:]:
                    most = jnp.maximum(most, part)
                most = jnp.max(most, axis=1, keepdims=True)
                weights = jnp.concatenate(
                    [jnp.exp2((part - most) * scale).astype(jnp.bfloat16) for part in parts], axis=1
                )
                both = mm(weights, vbuf[pl.ds(at, window), :])
                contexts.append((both[:, :width] / both[:, width:]).astype(jnp.bfloat16))
            context = jnp.concatenate(contexts, axis=0)
            back = mm(table_from(slot_ref[pl.ds(b, 1), :]), context).astype(jnp.bfloat16)
            out_ref[...] = back.reshape(senders, per, width)

    return pl.pallas_call(
        kernel,
        name="attend",
        grid_spec=pltpu.PrefetchScalarGridSpec(
            num_scalar_prefetch=1,
            grid=(nb + lag,),
            in_specs=[
                pl.BlockSpec((nb, rows), lambda g, p: (0, 0)),
                *[
                    pl.BlockSpec(
                        (senders, per, width),
                        lambda g, p, i=i: (0, i * nb + jnp.minimum(g, nb - 1), 0),
                    )
                    for i in range(3)
                ],
            ],
            out_specs=pl.BlockSpec((senders, per, width), lambda g, p: (0, jnp.maximum(g - lag, 0), 0)),
            scratch_shapes=[
                pltpu.VMEM((total, width), jnp.bfloat16),
                pltpu.VMEM((total, 2 * width), jnp.bfloat16),
                pltpu.VMEM((2, rows, width), jnp.bfloat16),
            ],
        ),
        out_shape=jax.ShapeDtypeStruct((senders, nb * per, width), jnp.bfloat16),
    )(pattern, slots, arrived, arrived, arrived)


def unpack(order, returned):
    heads, rows, width = returned.shape

    def kernel(order_ref, in_ref, out_ref):
        out_ref[...] = mm(table_from(order_ref[0]), in_ref[0]).astype(jnp.bfloat16)

    return pl.pallas_call(
        kernel,
        name="unpack",
        grid=(heads,),
        in_specs=[
            pl.BlockSpec((1, 1, rows), lambda h: (h, 0, 0)),
            pl.BlockSpec((1, rows, width), lambda h: (h, 0, 0)),
        ],
        out_specs=pl.BlockSpec((rows, width), lambda h: (0, h)),
        out_shape=jax.ShapeDtypeStruct((rows, heads * width), jnp.bfloat16),
    )(order, returned)


def project(pieces, pieces_too, attended, first, second):
    count = pieces.shape[0]
    rows, depth = attended.shape
    half, cols = first.shape[1:]

    def kernel(at_ref, too_ref, a_ref, f_ref, s_ref, out_ref):
        out_ref[...] = (mm(a_ref[:, :half], f_ref[0]) + mm(a_ref[:, half:], s_ref[0])).astype(
            jnp.bfloat16
        )

    return pl.pallas_call(
        kernel,
        name="project",
        grid_spec=pltpu.PrefetchScalarGridSpec(
            num_scalar_prefetch=2,
            grid=(count,),
            in_specs=[
                pl.BlockSpec((rows, depth), lambda j, at, too: (0, 0)),
                pl.BlockSpec((1, half, cols), lambda j, at, too: (at[j], 0, 0)),
                pl.BlockSpec((1, half, cols), lambda j, at, too: (too[j], 0, 0)),
            ],
            out_specs=pl.BlockSpec((rows, cols), lambda j, at, too: (0, j)),
        ),
        out_shape=jax.ShapeDtypeStruct((rows, count * cols), jnp.bfloat16),
    )(pieces, pieces_too, attended, first, second)


def gather_weights(w_out):
    count = lax.axis_size("seq")
    line = count // 4
    me = lax.axis_index("seq")
    moves = {
        "right": [(i, i + 4) for i in range(count - 4)],
        "left": [(i + 4, i) for i in range(count - 4)],
        "x": [(i, i ^ 1) for i in range(count)],
        "y": [(i, i ^ 2) for i in range(count)],
    }

    def moved(cells, way):
        return lax.ppermute(cells, "seq", moves[way])

    half = w_out.shape[0] // 2
    own = (w_out[None, :half], w_out[None, half:])
    from_left, from_right = [w_out], [w_out]
    from_left.append(moved(w_out, "right"))
    from_right.append(moved(w_out, "left"))
    ways = (("y", "x"), ("x", "y"))

    def spread(cells):
        both = []
        for color in range(2):
            there = moved(cells[color], ways[color][0])
            two = jnp.concatenate([cells[color], there], axis=0)
            both.append((two, moved(two, ways[color][1])))
        return both

    near = spread(own)
    for _ in range(2, line):
        from_left.append(moved(from_left[-1], "right"))
        from_right.append(moved(from_right[-1], "left"))
    rest = [from_left[k] + from_right[line - k] for k in range(1, line)]
    far = spread(
        (jnp.stack([cell[:half] for cell in rest]), jnp.stack([cell[half:] for cell in rest]))
    )
    stacks = [jnp.concatenate([*near[color], *far[color]], axis=0) for color in range(2)]
    names = jnp.arange(count, dtype=jnp.int32)
    step = jnp.mod(me // 4 - names // 4, line)
    differ = jnp.bitwise_xor(me, names)
    x_bit, y_bit = differ % 2, (differ // 2) % 2

    def place(inner, outer):
        return jnp.where(
            step == 0,
            outer * 2 + inner,
            4 + (outer * 2 + inner) * (line - 1) + step - 1,
        )

    return stacks, (place(y_bit, x_bit), place(x_bit, y_bit)), from_left[2]


def head_shards(queries, keys, values, route, members, pattern, w_out):
    heads, rows = route.shape
    count = lax.axis_size("seq")
    entries = pattern.shape[1] * pattern.shape[2]
    pattern = jnp.pad(pattern.reshape(heads, entries), ((0, 0), (0, LANES - entries)))
    stacks, places, hop = gather_weights(w_out)
    packed, order = pack(route, pattern, queries, keys, values)
    packed, _ = lax.optimization_barrier((packed, hop))
    arrived = lax.all_to_all(packed, "seq", split_axis=0, concat_axis=0, tiled=True)
    slots, pattern = tail_of(arrived, rows, entries)
    context = attend(slots, pattern, arrived)
    returned = lax.all_to_all(context, "seq", split_axis=0, concat_axis=0, tiled=True)
    attended = unpack(order, returned)
    mine = lax.axis_index("tp")
    half = count // 2

    def part(which):
        at = [lax.dynamic_slice_in_dim(place, which * half, half) for place in places]
        return project(at[0], at[1], attended, stacks[0], stacks[1])

    send = part(1 - mine)
    received = lax.ppermute(send, "tp", [(0, 1), (1, 0)])
    keep = part(mine)
    return (keep.astype(jnp.float32) + received.astype(jnp.float32)).astype(jnp.bfloat16)


def choose(mesh):
    count, groups = mesh.shape["seq"], mesh.shape["tp"]

    def shards(queries, keys, values, route, members, pattern, w_out):
        heads, rows = route.shape
        split = heads == count and groups == 2 and count % 4 == 0
        tiles = rows == REACH * CLUSTER and queries.shape[1] == heads * LANES
        body = head_shards if split and tiles else slot_shards
        return body(queries, keys, values, route, members, pattern, w_out)

    return shards


def solution(mesh):
    placed = (
        P("seq", "tp"),
        P("seq", "tp"),
        P("seq", "tp"),
        P("tp", "seq"),
        P("tp", "seq"),
        P("tp", "seq", None),
        P("tp", "seq"),
    )
    return jax.shard_map(
        choose(mesh), mesh=mesh, in_specs=placed, out_specs=P("seq", "tp"), check_vma=False
    )
```

```python
import jax
import jax.numpy as jnp
from jax import lax
from jax.experimental import pallas as pl
from jax.experimental.pallas import tpu as pltpu
from jax.sharding import PartitionSpec as P


CLUSTER = 256
REACH = 2


def extended_2(cells, sides, width):
    for axis, dim in sides:
        count = lax.axis_size(axis)
        ends = count - 1
        head = lax.slice_in_dim(cells, 0, width, axis=dim)
        tail = lax.slice_in_dim(cells, cells.shape[dim] - width, cells.shape[dim], axis=dim)
        cells = jnp.concatenate(
            [
                lax.ppermute(tail, axis, [(i, (i + 1) % count) for i in range(ends)]),
                cells,
                lax.ppermute(head, axis, [((i + 1) % count, i) for i in range(ends)]),
            ],
            axis=dim,
        )
    return cells


def attend_head(pieces):
    query_rows, key_rows, value_rows, pattern_rows = pieces
    head_width = query_rows.shape[1]
    cluster_count = query_rows.shape[0] // CLUSTER
    window_rows = (2 * REACH + 1) * CLUSTER
    starts = jnp.arange(cluster_count) * CLUSTER
    key_window = jax.vmap(
        lambda slot_start: lax.dynamic_slice_in_dim(key_rows, slot_start, window_rows, 0)
    )(starts)
    value_window = jax.vmap(
        lambda slot_start: lax.dynamic_slice_in_dim(value_rows, slot_start, window_rows, 0)
    )(starts)
    query_blocks = query_rows.reshape(cluster_count, CLUSTER, head_width)
    scores = jnp.einsum(
        "cqd,ckd->cqk", query_blocks, key_window, preferred_element_type=jnp.float32
    ) * head_width ** (-0.5)
    allowed = jnp.repeat(pattern_rows, CLUSTER // 2, axis=1) > 0
    scores = jnp.where(allowed[:, None, :], scores, -jnp.inf)
    row_max = jnp.max(scores, axis=-1, keepdims=True)
    exponent = jnp.exp(scores - row_max)
    weights = (exponent / jnp.sum(exponent, axis=-1, keepdims=True)).astype(jnp.bfloat16)
    context = jnp.einsum(
        "cqk,ckd->cqd", weights, value_window, preferred_element_type=jnp.float32
    ).astype(jnp.bfloat16)
    return context.reshape(query_rows.shape[0], head_width)


def buffer_index(group_of, order_key, per_peer):
    same_group = group_of[:, :, None] == group_of[:, None, :]
    earlier = order_key[:, None, :] < order_key[:, :, None]
    rank = jnp.sum((same_group & earlier).astype(jnp.int32), axis=2)
    return group_of * per_peer + rank


def slot_shards(queries, keys, values, route, members, pattern, w_out):
    rows_here = queries.shape[0]
    head_count = route.shape[0]
    head_width = queries.shape[1] // head_count
    peer_count = lax.axis_size("seq")
    per_peer = rows_here // peer_count
    local_iota = jnp.arange(rows_here, dtype=jnp.int32)
    send_index = buffer_index(route // rows_here, route, per_peer)
    local_slots = jnp.broadcast_to(local_iota[None, :], members.shape)
    arrival_index = buffer_index(members // rows_here, local_slots, per_peer)
    send_table = (send_index[:, None, :] == local_iota[None, :, None]).astype(jnp.bfloat16)
    land_table = (arrival_index[:, :, None] == local_iota[None, None, :]).astype(jnp.bfloat16)
    stacked = jnp.concatenate(
        [
            queries.reshape(rows_here, head_count, head_width),
            keys.reshape(rows_here, head_count, head_width),
            values.reshape(rows_here, head_count, head_width),
        ],
        axis=2,
    )
    packed = jnp.einsum(
        "hap,phd->had", send_table, stacked, preferred_element_type=jnp.float32
    ).astype(jnp.bfloat16)

    def outgoing(column_index):
        part_rows = packed[:, :, column_index * head_width : (column_index + 1) * head_width]
        return part_rows.reshape(head_count, peer_count, per_peer, head_width)

    sent_query, sent_key, sent_value = (
        lax.all_to_all(outgoing(0), "seq", split_axis=1, concat_axis=1, tiled=True),
        lax.all_to_all(outgoing(1), "seq", split_axis=1, concat_axis=1, tiled=True),
        lax.all_to_all(outgoing(2), "seq", split_axis=1, concat_axis=1, tiled=True),
    )
    arrived = jnp.concatenate(
        [
            sent_query.reshape(head_count, rows_here, head_width),
            sent_key.reshape(head_count, rows_here, head_width),
            sent_value.reshape(head_count, rows_here, head_width),
        ],
        axis=2,
    )
    placed = jnp.einsum(
        "hsa,had->hsd", land_table, arrived, preferred_element_type=jnp.float32
    ).astype(jnp.bfloat16)
    ordered_query = placed[:, :, :head_width]
    keys_values = jnp.stack(
        [placed[:, :, head_width : 2 * head_width], placed[:, :, 2 * head_width :]]
    )
    extended = extended_2(keys_values, (("seq", 2),), REACH * CLUSTER)
    context = lax.map(attend_head, (ordered_query, extended[0], extended[1], pattern))
    returning = jnp.einsum(
        "hsa,hsd->had", land_table, context, preferred_element_type=jnp.float32
    ).astype(jnp.bfloat16)
    returning = returning.reshape(head_count, peer_count, per_peer, head_width)
    returned = lax.all_to_all(returning, "seq", split_axis=1, concat_axis=1, tiled=True).reshape(
        head_count, rows_here, head_width
    )
    attended = jnp.einsum(
        "hap,had->phd", send_table, returned, preferred_element_type=jnp.float32
    ).astype(jnp.bfloat16)
    attended = attended.reshape(rows_here, head_count * head_width)
    partial_value = jnp.dot(
        attended,
        lax.all_gather(w_out, "seq", axis=1, tiled=True),
        preferred_element_type=jnp.float32,
    )
    mixed_out = lax.psum_scatter(
        partial_value.astype(jnp.bfloat16), "tp", scatter_dimension=1, tiled=True
    )
    return mixed_out


LANES = 128
DIGIT = 4
TAIL = 32
BLOCK = 128


def order_of(key_row):
    n = key_row.shape[1]
    key_col = jnp.broadcast_to(key_row, (LANES, n)).T
    counts = []
    for j in range(n // LANES):
        less = key_col < key_row[:, j * LANES : (j + 1) * LANES]
        counts.append(jnp.sum(jnp.where(less, 1, 0), axis=0, keepdims=True))
    return jnp.concatenate(counts, axis=1)


def table_to(order_row, first, last):
    n = order_row.shape[1]
    rows = lax.broadcasted_iota(jnp.int32, (last - first, n), 0) + first
    return jnp.where(rows == order_row, 1.0, 0.0).astype(jnp.bfloat16)


def table_from(order_row, first, last):
    n = order_row.shape[1]
    order_col = jnp.broadcast_to(order_row, (LANES, n)).T
    parts = []
    for start in range(first, last, LANES):
        lane = lax.broadcasted_iota(jnp.int32, (n, min(LANES, last - start)), 1) + start
        parts.append(jnp.where(order_col[:, : lane.shape[1]] == lane, 1.0, 0.0).astype(jnp.bfloat16))
    return jnp.concatenate(parts, axis=1) if len(parts) > 1 else parts[0]


def mm(a, b):
    return jnp.dot(a, b, preferred_element_type=jnp.float32)


def pack(route, pattern, queries, keys, values, first, last, order=None):
    heads, rows = route.shape
    width = queries.shape[1] // heads
    lines = rows // LANES
    leads = order is None
    part = last - first
    group = 2

    def emit(i, order_row, refs, out_ref):
        stacked = jnp.concatenate([ref[:, i * width : (i + 1) * width] for ref in refs], axis=1)
        put = mm(table_to(order_row, first, last), stacked).astype(jnp.bfloat16)
        for n in range(3):
            out_ref[i, n * part : (n + 1) * part] = put[:, n * width : (n + 1) * width]

    def lead(route_ref, pat_ref, q_ref, k_ref, v_ref, out_ref, order_ref):
        for i in range(group):
            h = pl.program_id(0) * group + i
            row = route_ref[pl.ds(h, 1), :]
            order_row = order_of(row)
            order_ref[i] = order_row
            emit(i, order_row, (q_ref, k_ref, v_ref), out_ref)
            slot = jnp.bitwise_and(row, rows - 1)
            high = lax.shift_right_logical(slot, DIGIT)
            low = jnp.bitwise_and(slot, (1 << DIGIT) - 1)
            at = lax.broadcasted_iota(jnp.int32, (8, rows), 0)
            digits = jnp.where(at == 0, high, jnp.where(at == 1, low, 0))
            digits = digits.astype(jnp.float32).astype(jnp.bfloat16)
            sorted_digits = lax.dot_general(
                digits,
                table_to(order_row, 0, rows),
                (((1,), (1,)), ((), ())),
                preferred_element_type=jnp.float32,
            )
            parts = [
                sorted_digits[d : d + 1, j * LANES : (j + 1) * LANES]
                for d in range(2)
                for j in range(lines)
            ]
            parts.append(pat_ref[pl.ds(h, 1), :].astype(jnp.float32))
            parts.append(jnp.zeros((TAIL - 2 * lines - 1, LANES), jnp.float32))
            out_ref[i, 3 * part :] = jnp.concatenate(parts, axis=0).astype(jnp.bfloat16)

    def follow(order_ref, q_ref, k_ref, v_ref, out_ref):
        for i in range(group):
            emit(i, order_ref[i], (q_ref, k_ref, v_ref), out_ref)

    columns = pl.BlockSpec((rows, group * width), lambda h: (0, h))
    order_spec = pl.BlockSpec((group, 1, rows), lambda h: (h, 0, 0))
    total = 3 * part + (TAIL if leads else 0)
    out_spec = pl.BlockSpec((group, total, width), lambda h: (h, 0, 0))
    out_shape = jax.ShapeDtypeStruct((heads, total, width), jnp.bfloat16)
    if not leads:
        return pl.pallas_call(
            follow,
            name="pack_rest",
            grid=(heads // group,),
            in_specs=[order_spec, columns, columns, columns],
            out_specs=out_spec,
            out_shape=out_shape,
        )(order, queries, keys, values)
    return pl.pallas_call(
        lead,
        name="pack",
        grid=(heads // group,),
        in_specs=[
            pl.BlockSpec((heads, rows), lambda h: (0, 0)),
            pl.BlockSpec((heads, LANES), lambda h: (0, 0)),
            columns,
            columns,
            columns,
        ],
        out_specs=[out_spec, order_spec],
        out_shape=[out_shape, jax.ShapeDtypeStruct((heads, 1, rows), jnp.int32)],
    )(route, pattern, queries, keys, values)


def tail_of(arrived, rows, entries):
    senders = arrived.shape[0]
    lines = rows // LANES
    tail = arrived[:, -TAIL:].astype(jnp.int32)
    slot = (tail[:, :lines] << DIGIT) + tail[:, lines : 2 * lines]
    slot = slot.reshape(senders, senders, rows // senders).transpose(1, 0, 2)
    return slot.reshape(senders, rows), tail[:, 2 * lines, :entries].reshape(-1)


def attend(slots, pattern, arrived, count, kept=None):
    nb, rows = slots.shape
    senders, _, width = arrived.shape
    per = rows // senders
    per_block = rows // CLUSTER
    window = (2 * REACH + 1) * CLUSTER
    blocks = window // BLOCK
    leads = kept is None
    lowest = 0 if leads else nb - count
    steps = count if leads else count + 1
    done = count - 1 if leads else count + 1
    ahead = rows if leads else 2 * rows
    total = (count + (1 if leads else 3)) * rows
    scale = width ** (-0.5) * 1.4426950408889634

    def kernel(pat_ref, slot_ref, q_ref, k_ref, v_ref, *refs):
        if leads:
            out_ref, q_keep, k_keep, v_keep, kbuf, vbuf, qbuf = refs
        else:
            q_kept, k_kept, v_kept, out_ref, kbuf, vbuf, qbuf = refs
        g = pl.program_id(0)

        @pl.when(g == 0)
        def _():
            zero = jnp.zeros((rows, width), jnp.bfloat16)
            vbuf[:, width:] = jnp.ones((total, width), jnp.bfloat16)
            if leads:
                kbuf[:rows, :] = zero
                vbuf[:rows, :width] = zero
            else:
                kbuf[: 2 * rows, :] = k_kept[...]
                vbuf[: 2 * rows, :width] = v_kept[...]
                qbuf[(lowest - 1) % 2] = q_kept[...]
                kbuf[total - rows :, :] = zero
                vbuf[total - rows :, :width] = zero

        @pl.when(g < count)
        def _():
            block = g + lowest
            table = table_to(slot_ref[pl.ds(block, 1), :], 0, rows)
            at = pl.multiple_of(g * rows + ahead, rows)
            put = [
                mm(table, ref[...].reshape(rows, width)).astype(jnp.bfloat16)
                for ref in (q_ref, k_ref, v_ref)
            ]
            qbuf[pl.ds(block % 2, 1)] = put[0][None]
            kbuf[pl.ds(at, rows), :] = put[1]
            vbuf[pl.ds(at, rows), :width] = put[2]
            if leads:

                @pl.when(g == count - 1)
                def _():
                    q_keep[...] = put[0]
                    k_keep[:rows, :] = kbuf[total - 2 * rows : total - rows, :]
                    v_keep[:rows, :] = vbuf[total - 2 * rows : total - rows, :width]
                    k_keep[rows:, :] = put[1]
                    v_keep[rows:, :] = put[2]

        @pl.when(g + lowest > 0)
        def _():
            b = g + lowest - 1
            base = (g - 1 if leads else g) * rows
            contexts = []
            for i in range(per_block):
                q = qbuf[pl.ds(b % 2, 1), i * CLUSTER : (i + 1) * CLUSTER, :][0]
                at = pl.multiple_of(base + i * CLUSTER, CLUSTER)
                scores = lax.dot_general(
                    q,
                    kbuf[pl.ds(at, window), :],
                    (((1,), (1,)), ((), ())),
                    preferred_element_type=jnp.float32,
                )
                parts = []
                for j in range(blocks):
                    allowed = pat_ref[(b * per_block + i) * blocks + j] > 0
                    shift = jnp.where(allowed, 0.0, -jnp.inf)
                    parts.append(scores[:, j * BLOCK : (j + 1) * BLOCK] + shift)
                most = parts[0]
                for part in parts[1:]:
                    most = jnp.maximum(most, part)
                most = jnp.max(most, axis=1, keepdims=True)
                weights = jnp.concatenate(
                    [jnp.exp2((part - most) * scale).astype(jnp.bfloat16) for part in parts], axis=1
                )
                both = mm(weights, vbuf[pl.ds(at, window), :])
                contexts.append((both[:, :width] / both[:, width:]).astype(jnp.bfloat16))
            context = jnp.concatenate(contexts, axis=0)
            back = mm(table_from(slot_ref[pl.ds(b, 1), :], 0, rows), context).astype(jnp.bfloat16)
            out_ref[...] = back.reshape(senders, per, width)

    whole = lambda *shape: pl.BlockSpec(shape, lambda g, p: (0,) * len(shape))
    incoming = [
        pl.BlockSpec(
            (senders, per, width), lambda g, p, i=i: (0, i * count + jnp.minimum(g, count - 1), 0)
        )
        for i in range(3)
    ]
    keep_specs = [whole(rows, width), whole(2 * rows, width), whole(2 * rows, width)]
    out_specs = [
        pl.BlockSpec(
            (senders, per, width), lambda g, p: (0, jnp.maximum(g - 1, 0) if leads else g, 0)
        )
    ]
    out_shape = [jax.ShapeDtypeStruct((senders, done * per, width), jnp.bfloat16)]
    if leads:
        out_specs += keep_specs
        out_shape += [
            jax.ShapeDtypeStruct((n * rows, width), jnp.bfloat16) for n in (1, 2, 2)
        ]
    out = pl.pallas_call(
        kernel,
        name="attend" if leads else "attend_rest",
        grid_spec=pltpu.PrefetchScalarGridSpec(
            num_scalar_prefetch=1,
            grid=(steps,),
            in_specs=[whole(nb, rows), *incoming] + ([] if leads else keep_specs),
            out_specs=out_specs,
            scratch_shapes=[
                pltpu.VMEM((total, width), jnp.bfloat16),
                pltpu.VMEM((total, 2 * width), jnp.bfloat16),
                pltpu.VMEM((2, rows, width), jnp.bfloat16),
            ],
        ),
        out_shape=out_shape,
    )(pattern, slots, arrived, arrived, arrived, *(() if leads else kept))
    return out[0], out[1:]


def unpack(order, returned, first, last, partial=None):
    heads, _, width = returned.shape
    rows = order.shape[2]
    group = 4

    def kernel(order_ref, in_ref, *refs):
        for i in range(group):
            put = mm(table_from(order_ref[i], first, last), in_ref[i]).astype(jnp.bfloat16)
            at = slice(i * width, (i + 1) * width)
            if partial is not None:
                put = put + refs[0][:, at]
            refs[-1][:, at] = put

    columns = pl.BlockSpec((rows, group * width), lambda h: (0, h))
    return pl.pallas_call(
        kernel,
        name="unpack" if partial is None else "unpack_rest",
        grid=(heads // group,),
        in_specs=[
            pl.BlockSpec((group, 1, rows), lambda h: (h, 0, 0)),
            pl.BlockSpec((group, last - first, width), lambda h: (h, 0, 0)),
        ]
        + ([] if partial is None else [columns]),
        out_specs=columns,
        out_shape=jax.ShapeDtypeStruct((rows, heads * width), jnp.bfloat16),
    )(order, returned, *(() if partial is None else (partial,)))


def project(places, attended, cells, received=None, start=0, into=None):
    count = places.shape[1]
    rows, depth = attended.shape
    halves, kinds = len(cells), len(cells[0])
    half, cols = cells[0][0].shape[1:]

    def kernel(at_ref, a_ref, *refs):
        arrays = [refs[c * kinds : (c + 1) * kinds] for c in range(halves)]
        rest = refs[halves * kinds :]
        buffer, sems = rest[-2:]
        out_ref = rest[-3]
        j = pl.program_id(0)

        def copy(p, c, source):
            to = buffer.at[p // 2, pl.ds(c * half, half), pl.ds(p % 2 * cols, cols)]
            return pltpu.make_async_copy(source, to, sems.at[p, c])

        @pl.when(j == 0)
        def _():
            for p in range(count):
                for c in range(halves):
                    for kind in range(kinds):

                        @pl.when(at_ref[2 * c, p] == kind)
                        def _():
                            copy(p, c, arrays[c][kind].at[at_ref[2 * c + 1, p]]).start()

        for p in range(count):

            @pl.when(j == p // 2)
            def _():
                for c in range(halves):
                    copy(p, c, arrays[c][0].at[0]).wait()

        value = mm(a_ref[...], buffer[pl.ds(j, 1)][0])
        if received is not None:
            value = value + rest[0][...].astype(jnp.float32)
        out_ref[...] = value.astype(jnp.bfloat16)

    anywhere = pl.BlockSpec(memory_space=pl.ANY)
    in_specs = [pl.BlockSpec((rows, depth), lambda j, at: (0, 0))] + [anywhere] * (halves * kinds)
    args = [attended] + [cell for group in cells for cell in group]
    width = count * cols
    if received is not None:
        in_specs.append(pl.BlockSpec((rows, 2 * cols), lambda j, at: (0, j)))
        args.append(received)
        width = 2 * width
    if into is not None:
        in_specs.append(anywhere)
        args.append(into)
    return pl.pallas_call(
        kernel,
        name="project",
        grid_spec=pltpu.PrefetchScalarGridSpec(
            num_scalar_prefetch=1,
            grid=(count // 2,),
            in_specs=in_specs,
            out_specs=pl.BlockSpec((rows, 2 * cols), lambda j, at: (0, j + start)),
            scratch_shapes=[
                pltpu.VMEM((count // 2, depth, 2 * cols), jnp.bfloat16),
                pltpu.SemaphoreType.DMA((count, halves)),
            ],
        ),
        out_shape=jax.ShapeDtypeStruct((rows, width), jnp.bfloat16),
        input_output_aliases={} if into is None else {len(args): 0},
    )(places, *args)


def gather_weights(w_out):
    count = lax.axis_size("seq")
    line = count // 4
    me = lax.axis_index("seq")
    moves = {
        "right": [(i, i + 4) for i in range(count - 4)],
        "left": [(i + 4, i) for i in range(count - 4)],
        "x": [(i, i ^ 1) for i in range(count)],
        "y": [(i, i ^ 2) for i in range(count)],
    }

    def moved(cells, way):
        return lax.ppermute(cells, "seq", moves[way])

    half = w_out.shape[0] // 2
    own = (w_out[None, :half], w_out[None, half:])
    from_left, from_right = [w_out], [w_out]
    from_left.append(moved(w_out, "right"))
    from_right.append(moved(w_out, "left"))
    ways = (("y", "x"), ("x", "y"))

    def spread(cells):
        both = []
        for color in range(2):
            there = moved(cells[color], ways[color][0])
            two = jnp.concatenate([cells[color], there], axis=0)
            both.append((two, moved(two, ways[color][1])))
        return both

    near = spread(own)
    for _ in range(2, line):
        from_left.append(moved(from_left[-1], "right"))
        from_right.append(moved(from_right[-1], "left"))
    middle = from_left[2] + from_right[2]
    middle = [middle[None, :half], middle[None, half:]]
    mid = spread(middle)
    ends = [from_left[1] + from_right[3], from_left[3] + from_right[1]]
    ends = [jnp.stack([cell[at : at + half] for cell in ends]) for at in (0, half)]
    far = spread(ends)
    cells = [[*near[c], *mid[c], *far[c]] for c in range(2)]
    names = jnp.arange(count, dtype=jnp.int32)
    step = jnp.mod(me // 4 - names // 4, line)
    odd = step & 1
    group = jnp.where(step == 0, 0, 1 + odd)
    differ = jnp.bitwise_xor(me, names)
    x_bit, y_bit = differ & 1, (differ >> 1) & 1
    places = []
    for inner, outer in ((y_bit, x_bit), (x_bit, y_bit)):
        places.append(outer + 2 * group)
        places.append(jnp.where(odd == 1, inner * 2 + (step >> 1), inner))
    return cells, jnp.stack(places)


def head_shards(queries, keys, values, route, members, pattern, w_out):
    heads, rows = route.shape
    count = lax.axis_size("seq")
    per = rows // count
    entries = pattern.shape[1] * pattern.shape[2]
    early = count // 2
    cut, cut_back = early * per, (early - 1) * per
    pattern = jnp.pad(pattern.reshape(heads, entries), ((0, 0), (0, LANES - entries)))

    def exchange(cells):
        return lax.all_to_all(cells, "seq", split_axis=0, concat_axis=0, tiled=True)

    cells, place = gather_weights(w_out)
    packed, order = pack(route, pattern, queries, keys, values, 0, cut)
    packed_rest = pack(route, pattern, queries, keys, values, cut, rows, order)
    arrived = exchange(packed)
    arrived_rest = exchange(packed_rest)
    slots, pattern = tail_of(arrived, rows, entries)
    context, kept = attend(slots, pattern, arrived, early)
    returned = exchange(context)
    context_rest, _ = attend(slots, pattern, arrived_rest, count - early, kept)
    returned_rest = exchange(context_rest)
    attended = unpack(order, returned, 0, cut_back)
    attended = unpack(order, returned_rest, cut_back, rows, attended)
    mine = lax.axis_index("tp")
    quarter = count // 4

    def places(which, part):
        return lax.dynamic_slice_in_dim(place, (which * 2 + part) * quarter, quarter, 1)

    received = []
    for part in range(2):
        send = project(places(1 - mine, part), attended, cells)
        received.append(lax.ppermute(send, "tp", [(0, 1), (1, 0)]))
    mixed = None
    for part in range(2):
        mixed = project(
            places(mine, part), attended, cells, received[part], part * quarter // 2, mixed
        )
    return mixed


def choose(mesh):
    count, groups = mesh.shape["seq"], mesh.shape["tp"]

    def shards(queries, keys, values, route, members, pattern, w_out):
        heads, rows = route.shape
        split = heads == count and groups == 2 and count == 4 * 4
        tiles = rows == REACH * CLUSTER and queries.shape[1] == heads * LANES
        body = head_shards if split and tiles else slot_shards
        return body(queries, keys, values, route, members, pattern, w_out)

    return shards


def solution(mesh):
    placed = (
        P("seq", "tp"),
        P("seq", "tp"),
        P("seq", "tp"),
        P("tp", "seq"),
        P("tp", "seq"),
        P("tp", "seq", None),
        P("tp", "seq"),
    )
    return jax.shard_map(
        choose(mesh), mesh=mesh, in_specs=placed, out_specs=P("seq", "tp"), check_vma=False
    )
```

```python
import jax
import jax.numpy as jnp
from jax import lax
from jax.experimental import pallas as pl
from jax.experimental.pallas import tpu as pltpu
from jax.sharding import PartitionSpec as P


CLUSTER = 256
REACH = 2


def extended_2(cells, sides, width):
    for axis, dim in sides:
        count = lax.axis_size(axis)
        ends = count - 1
        head = lax.slice_in_dim(cells, 0, width, axis=dim)
        tail = lax.slice_in_dim(cells, cells.shape[dim] - width, cells.shape[dim], axis=dim)
        cells = jnp.concatenate(
            [
                lax.ppermute(tail, axis, [(i, (i + 1) % count) for i in range(ends)]),
                cells,
                lax.ppermute(head, axis, [((i + 1) % count, i) for i in range(ends)]),
            ],
            axis=dim,
        )
    return cells


def attend_head(pieces):
    query_rows, key_rows, value_rows, pattern_rows = pieces
    head_width = query_rows.shape[1]
    cluster_count = query_rows.shape[0] // CLUSTER
    window_rows = (2 * REACH + 1) * CLUSTER
    starts = jnp.arange(cluster_count) * CLUSTER
    key_window = jax.vmap(
        lambda slot_start: lax.dynamic_slice_in_dim(key_rows, slot_start, window_rows, 0)
    )(starts)
    value_window = jax.vmap(
        lambda slot_start: lax.dynamic_slice_in_dim(value_rows, slot_start, window_rows, 0)
    )(starts)
    query_blocks = query_rows.reshape(cluster_count, CLUSTER, head_width)
    scores = jnp.einsum(
        "cqd,ckd->cqk", query_blocks, key_window, preferred_element_type=jnp.float32
    ) * head_width ** (-0.5)
    allowed = jnp.repeat(pattern_rows, CLUSTER // 2, axis=1) > 0
    scores = jnp.where(allowed[:, None, :], scores, -jnp.inf)
    row_max = jnp.max(scores, axis=-1, keepdims=True)
    exponent = jnp.exp(scores - row_max)
    weights = (exponent / jnp.sum(exponent, axis=-1, keepdims=True)).astype(jnp.bfloat16)
    context = jnp.einsum(
        "cqk,ckd->cqd", weights, value_window, preferred_element_type=jnp.float32
    ).astype(jnp.bfloat16)
    return context.reshape(query_rows.shape[0], head_width)


def buffer_index(group_of, order_key, per_peer):
    same_group = group_of[:, :, None] == group_of[:, None, :]
    earlier = order_key[:, None, :] < order_key[:, :, None]
    rank = jnp.sum((same_group & earlier).astype(jnp.int32), axis=2)
    return group_of * per_peer + rank


def slot_shards(queries, keys, values, route, members, pattern, w_out):
    rows_here = queries.shape[0]
    head_count = route.shape[0]
    head_width = queries.shape[1] // head_count
    peer_count = lax.axis_size("seq")
    per_peer = rows_here // peer_count
    local_iota = jnp.arange(rows_here, dtype=jnp.int32)
    send_index = buffer_index(route // rows_here, route, per_peer)
    local_slots = jnp.broadcast_to(local_iota[None, :], members.shape)
    arrival_index = buffer_index(members // rows_here, local_slots, per_peer)
    send_table = (send_index[:, None, :] == local_iota[None, :, None]).astype(jnp.bfloat16)
    land_table = (arrival_index[:, :, None] == local_iota[None, None, :]).astype(jnp.bfloat16)
    stacked = jnp.concatenate(
        [
            queries.reshape(rows_here, head_count, head_width),
            keys.reshape(rows_here, head_count, head_width),
            values.reshape(rows_here, head_count, head_width),
        ],
        axis=2,
    )
    packed = jnp.einsum(
        "hap,phd->had", send_table, stacked, preferred_element_type=jnp.float32
    ).astype(jnp.bfloat16)

    def outgoing(column_index):
        part_rows = packed[:, :, column_index * head_width : (column_index + 1) * head_width]
        return part_rows.reshape(head_count, peer_count, per_peer, head_width)

    sent_query, sent_key, sent_value = (
        lax.all_to_all(outgoing(0), "seq", split_axis=1, concat_axis=1, tiled=True),
        lax.all_to_all(outgoing(1), "seq", split_axis=1, concat_axis=1, tiled=True),
        lax.all_to_all(outgoing(2), "seq", split_axis=1, concat_axis=1, tiled=True),
    )
    arrived = jnp.concatenate(
        [
            sent_query.reshape(head_count, rows_here, head_width),
            sent_key.reshape(head_count, rows_here, head_width),
            sent_value.reshape(head_count, rows_here, head_width),
        ],
        axis=2,
    )
    placed = jnp.einsum(
        "hsa,had->hsd", land_table, arrived, preferred_element_type=jnp.float32
    ).astype(jnp.bfloat16)
    ordered_query = placed[:, :, :head_width]
    keys_values = jnp.stack(
        [placed[:, :, head_width : 2 * head_width], placed[:, :, 2 * head_width :]]
    )
    extended = extended_2(keys_values, (("seq", 2),), REACH * CLUSTER)
    context = lax.map(attend_head, (ordered_query, extended[0], extended[1], pattern))
    returning = jnp.einsum(
        "hsa,hsd->had", land_table, context, preferred_element_type=jnp.float32
    ).astype(jnp.bfloat16)
    returning = returning.reshape(head_count, peer_count, per_peer, head_width)
    returned = lax.all_to_all(returning, "seq", split_axis=1, concat_axis=1, tiled=True).reshape(
        head_count, rows_here, head_width
    )
    attended = jnp.einsum(
        "hap,had->phd", send_table, returned, preferred_element_type=jnp.float32
    ).astype(jnp.bfloat16)
    attended = attended.reshape(rows_here, head_count * head_width)
    partial_value = jnp.dot(
        attended,
        lax.all_gather(w_out, "seq", axis=1, tiled=True),
        preferred_element_type=jnp.float32,
    )
    mixed_out = lax.psum_scatter(
        partial_value.astype(jnp.bfloat16), "tp", scatter_dimension=1, tiled=True
    )
    return mixed_out


LANES = 128
DIGIT = 4
TAIL = 16
BLOCK = 128


def order_of(key_row):
    n = key_row.shape[1]
    key_col = jnp.broadcast_to(key_row, (LANES, n)).T
    counts = []
    for j in range(n // LANES):
        less = key_col < key_row[:, j * LANES : (j + 1) * LANES]
        counts.append(jnp.sum(jnp.where(less, 1, 0), axis=0, keepdims=True))
    return jnp.concatenate(counts, axis=1)


def table_to(order_row, first, last):
    n = order_row.shape[1]
    rows = lax.broadcasted_iota(jnp.int32, (last - first, n), 0) + first
    return jnp.where(rows == order_row, 1.0, 0.0).astype(jnp.bfloat16)


def table_from(order_row, first, last):
    n = order_row.shape[1]
    order_col = jnp.broadcast_to(order_row, (LANES, n)).T
    parts = []
    for start in range(first, last, LANES):
        lane = lax.broadcasted_iota(jnp.int32, (n, min(LANES, last - start)), 1) + start
        parts.append(jnp.where(order_col[:, : lane.shape[1]] == lane, 1.0, 0.0).astype(jnp.bfloat16))
    return jnp.concatenate(parts, axis=1) if len(parts) > 1 else parts[0]


def mm(a, b):
    return jnp.dot(a, b, preferred_element_type=jnp.float32)


def pack(route, pattern, queries, keys, values, first, last, order=None):
    heads, rows = route.shape
    width = queries.shape[1] // heads
    lines = rows // LANES
    leads = order is None
    part = last - first
    group = 2

    def emit(i, order_row, refs, out_ref):
        stacked = jnp.concatenate([ref[:, i * width : (i + 1) * width] for ref in refs], axis=1)
        put = mm(table_to(order_row, first, last), stacked).astype(jnp.bfloat16)
        for n in range(3):
            out_ref[i, n * part : (n + 1) * part] = put[:, n * width : (n + 1) * width]

    def lead(route_ref, pat_ref, q_ref, k_ref, v_ref, out_ref, order_ref):
        for i in range(group):
            h = pl.program_id(0) * group + i
            row = route_ref[pl.ds(h, 1), :]
            order_row = order_of(row)
            order_ref[i] = order_row
            emit(i, order_row, (q_ref, k_ref, v_ref), out_ref)
            slot = jnp.bitwise_and(row, rows - 1)
            high = lax.shift_right_logical(slot, DIGIT)
            low = jnp.bitwise_and(slot, (1 << DIGIT) - 1)
            at = lax.broadcasted_iota(jnp.int32, (8, rows), 0)
            digits = jnp.where(at == 0, high, jnp.where(at == 1, low, 0))
            digits = digits.astype(jnp.float32).astype(jnp.bfloat16)
            sorted_digits = lax.dot_general(
                digits,
                table_to(order_row, 0, rows),
                (((1,), (1,)), ((), ())),
                preferred_element_type=jnp.float32,
            )
            parts = [
                sorted_digits[d : d + 1, j * LANES : (j + 1) * LANES]
                for d in range(2)
                for j in range(lines)
            ]
            parts.append(pat_ref[pl.ds(h, 1), :].astype(jnp.float32))
            parts.append(jnp.zeros((TAIL - 2 * lines - 1, LANES), jnp.float32))
            out_ref[i, 3 * part :] = jnp.concatenate(parts, axis=0).astype(jnp.bfloat16)

    def follow(order_ref, q_ref, k_ref, v_ref, out_ref):
        for i in range(group):
            emit(i, order_ref[i], (q_ref, k_ref, v_ref), out_ref)

    columns = pl.BlockSpec((rows, group * width), lambda h: (0, h))
    order_spec = pl.BlockSpec((group, 1, rows), lambda h: (h, 0, 0))
    total = 3 * part + (TAIL if leads else 0)
    out_spec = pl.BlockSpec((group, total, width), lambda h: (h, 0, 0))
    out_shape = jax.ShapeDtypeStruct((heads, total, width), jnp.bfloat16)
    if not leads:
        return pl.pallas_call(
            follow,
            name="pack_rest",
            grid=(heads // group,),
            in_specs=[order_spec, columns, columns, columns],
            out_specs=out_spec,
            out_shape=out_shape,
        )(order, queries, keys, values)
    return pl.pallas_call(
        lead,
        name="pack",
        grid=(heads // group,),
        in_specs=[
            pl.BlockSpec((heads, rows), lambda h: (0, 0)),
            pl.BlockSpec((heads, LANES), lambda h: (0, 0)),
            columns,
            columns,
            columns,
        ],
        out_specs=[out_spec, order_spec],
        out_shape=[out_shape, jax.ShapeDtypeStruct((heads, 1, rows), jnp.int32)],
    )(route, pattern, queries, keys, values)


def tail_of(arrived, rows, entries):
    senders = arrived.shape[0]
    lines = rows // LANES
    tail = arrived[:, -TAIL:].astype(jnp.int32)
    slot = (tail[:, :lines] << DIGIT) + tail[:, lines : 2 * lines]
    slot = slot.reshape(senders, senders, rows // senders).transpose(1, 0, 2)
    return slot.reshape(senders, rows), tail[:, 2 * lines, :entries].reshape(-1)


def attend(slots, pattern, arrived, count, kept=None):
    nb, rows = slots.shape
    senders, _, width = arrived.shape
    per = rows // senders
    per_block = rows // CLUSTER
    window = (2 * REACH + 1) * CLUSTER
    blocks = window // BLOCK
    leads = kept is None
    lowest = 0 if leads else nb - count
    steps = count if leads else count + 1
    done = count - 1 if leads else count + 1
    ahead = rows if leads else 2 * rows
    total = (count + (1 if leads else 3)) * rows
    scale = width ** (-0.5) * 1.4426950408889634

    def kernel(pat_ref, slot_ref, q_ref, k_ref, v_ref, *refs):
        if leads:
            out_ref, q_keep, k_keep, v_keep, kbuf, vbuf, qbuf = refs
        else:
            q_kept, k_kept, v_kept, out_ref, kbuf, vbuf, qbuf = refs
        g = pl.program_id(0)

        @pl.when(g == 0)
        def _():
            zero = jnp.zeros((rows, width), jnp.bfloat16)
            vbuf[:, width:] = jnp.ones((total, width), jnp.bfloat16)
            if leads:
                kbuf[:rows, :] = zero
                vbuf[:rows, :width] = zero
            else:
                kbuf[: 2 * rows, :] = k_kept[...]
                vbuf[: 2 * rows, :width] = v_kept[...]
                qbuf[(lowest - 1) % 2] = q_kept[...]
                kbuf[total - rows :, :] = zero
                vbuf[total - rows :, :width] = zero

        @pl.when(g < count)
        def _():
            block = g + lowest
            table = table_to(slot_ref[pl.ds(block, 1), :], 0, rows)
            at = pl.multiple_of(g * rows + ahead, rows)
            put = [
                mm(table, ref[...].reshape(rows, width)).astype(jnp.bfloat16)
                for ref in (q_ref, k_ref, v_ref)
            ]
            qbuf[pl.ds(block % 2, 1)] = put[0][None]
            kbuf[pl.ds(at, rows), :] = put[1]
            vbuf[pl.ds(at, rows), :width] = put[2]
            if leads:

                @pl.when(g == count - 1)
                def _():
                    q_keep[...] = put[0]
                    k_keep[:rows, :] = kbuf[total - 2 * rows : total - rows, :]
                    v_keep[:rows, :] = vbuf[total - 2 * rows : total - rows, :width]
                    k_keep[rows:, :] = put[1]
                    v_keep[rows:, :] = put[2]

        @pl.when(g + lowest > 0)
        def _():
            b = g + lowest - 1
            base = (g - 1 if leads else g) * rows
            contexts = []
            for i in range(per_block):
                q = qbuf[pl.ds(b % 2, 1), i * CLUSTER : (i + 1) * CLUSTER, :][0]
                at = pl.multiple_of(base + i * CLUSTER, CLUSTER)
                scores = lax.dot_general(
                    q,
                    kbuf[pl.ds(at, window), :],
                    (((1,), (1,)), ((), ())),
                    preferred_element_type=jnp.float32,
                )
                parts = []
                for j in range(blocks):
                    allowed = pat_ref[(b * per_block + i) * blocks + j] > 0
                    shift = jnp.where(allowed, 0.0, -jnp.inf)
                    parts.append(scores[:, j * BLOCK : (j + 1) * BLOCK] + shift)
                most = parts[0]
                for part in parts[1:]:
                    most = jnp.maximum(most, part)
                most = jnp.max(most, axis=1, keepdims=True)
                weights = jnp.concatenate(
                    [jnp.exp2((part - most) * scale).astype(jnp.bfloat16) for part in parts], axis=1
                )
                both = mm(weights, vbuf[pl.ds(at, window), :])
                contexts.append((both[:, :width] / both[:, width:]).astype(jnp.bfloat16))
            context = jnp.concatenate(contexts, axis=0)
            back = mm(table_from(slot_ref[pl.ds(b, 1), :], 0, rows), context).astype(jnp.bfloat16)
            out_ref[...] = back.reshape(senders, per, width)

    whole = lambda *shape: pl.BlockSpec(shape, lambda g, p: (0,) * len(shape))
    incoming = [
        pl.BlockSpec(
            (senders, per, width), lambda g, p, i=i: (0, i * count + jnp.minimum(g, count - 1), 0)
        )
        for i in range(3)
    ]
    keep_specs = [whole(rows, width), whole(2 * rows, width), whole(2 * rows, width)]
    out_specs = [
        pl.BlockSpec(
            (senders, per, width), lambda g, p: (0, jnp.maximum(g - 1, 0) if leads else g, 0)
        )
    ]
    out_shape = [jax.ShapeDtypeStruct((senders, done * per, width), jnp.bfloat16)]
    if leads:
        out_specs += keep_specs
        out_shape += [
            jax.ShapeDtypeStruct((n * rows, width), jnp.bfloat16) for n in (1, 2, 2)
        ]
    out = pl.pallas_call(
        kernel,
        name="attend" if leads else "attend_rest",
        grid_spec=pltpu.PrefetchScalarGridSpec(
            num_scalar_prefetch=1,
            grid=(steps,),
            in_specs=[whole(nb, rows), *incoming] + ([] if leads else keep_specs),
            out_specs=out_specs,
            scratch_shapes=[
                pltpu.VMEM((total, width), jnp.bfloat16),
                pltpu.VMEM((total, 2 * width), jnp.bfloat16),
                pltpu.VMEM((2, rows, width), jnp.bfloat16),
            ],
        ),
        out_shape=out_shape,
    )(pattern, slots, arrived, arrived, arrived, *(() if leads else kept))
    return out[0], out[1:]


def unpack(order, returned, first, last):
    heads, _, width = returned.shape
    rows = order.shape[2]
    group = 4

    def kernel(order_ref, in_ref, out_ref):
        parts = [
            mm(table_from(order_ref[i], first, last), in_ref[i]).astype(jnp.bfloat16)
            for i in range(group)
        ]
        out_ref[...] = jnp.concatenate(parts, axis=1)

    return pl.pallas_call(
        kernel,
        name="unpack",
        grid=(heads // group,),
        in_specs=[
            pl.BlockSpec((group, 1, rows), lambda h: (h, 0, 0)),
            pl.BlockSpec((group, last - first, width), lambda h: (h, 0, 0)),
        ],
        out_specs=pl.BlockSpec((rows, group * width), lambda h: (0, h)),
        out_shape=jax.ShapeDtypeStruct((rows, heads * width), jnp.bfloat16),
    )(order, returned)


def fetcher(at_ref, arrays, buffer, sems):
    half, cols = arrays[0][0].shape[1:]

    def copy(p, c, source):
        to = buffer.at[p // 2, pl.ds(c * half, half), pl.ds(p % 2 * cols, cols)]
        return pltpu.make_async_copy(source, to, sems.at[p, c])

    def start(slot):
        for p in (2 * slot, 2 * slot + 1):
            for c, kinds in enumerate(arrays):
                for kind, array in enumerate(kinds):

                    @pl.when(at_ref[2 * c, p] == kind)
                    def _():
                        copy(p, c, array.at[at_ref[2 * c + 1, p]]).start()

    def wait(slot):
        for p in (2 * slot, 2 * slot + 1):
            for c, kinds in enumerate(arrays):
                copy(p, c, kinds[0].at[0]).wait()

    return start, wait


def fetch_scratch(count, cells):
    half, cols = cells[0][0].shape[1:]
    return [
        pltpu.VMEM((count // 2, len(cells) * half, 2 * cols), jnp.bfloat16),
        pltpu.SemaphoreType.DMA((count, len(cells))),
    ]


def split(refs, cells):
    kinds = len(cells[0])
    return [refs[c * kinds : (c + 1) * kinds] for c in range(len(cells))], refs[len(cells) * kinds :]


def project(places, attended, cells):
    slots = places.shape[1] // 2
    rows, depth = attended.shape
    wide = 2 * cells[0][0].shape[2]

    def kernel(at_ref, a_ref, *refs):
        arrays, (out_ref, buffer, sems) = split(refs, cells)
        start, wait = fetcher(at_ref, arrays, buffer, sems)
        j = pl.program_id(0)
        for slot in range(slots):

            @pl.when(j == max(slot - 2, 0))
            def _():
                start(slot)

        for slot in range(slots):

            @pl.when(j == slot)
            def _():
                wait(slot)

        out_ref[...] = mm(a_ref[...], buffer[pl.ds(j, 1)][0]).astype(jnp.bfloat16)

    flat = [cell for group in cells for cell in group]
    return pl.pallas_call(
        kernel,
        name="project",
        grid_spec=pltpu.PrefetchScalarGridSpec(
            num_scalar_prefetch=1,
            grid=(slots,),
            in_specs=[pl.BlockSpec((rows, depth), lambda j, at: (0, 0))]
            + [pl.BlockSpec(memory_space=pl.ANY)] * len(flat),
            out_specs=pl.BlockSpec((rows, wide), lambda j, at: (0, j)),
            scratch_shapes=fetch_scratch(2 * slots, cells),
        ),
        out_shape=jax.ShapeDtypeStruct((rows, slots * wide), jnp.bfloat16),
    )(places, attended, *flat)


def unpack_project(order, returned, first, last, partial, places, cells):
    heads, _, width = returned.shape
    rows = order.shape[2]
    slots = places.shape[1] // 2
    wide = 2 * cells[0][0].shape[2]
    group = 4
    turns = heads // group

    def kernel(at_ref, order_ref, in_ref, part_ref, *refs):
        arrays, (out_ref, att_ref, whole, buffer, sems) = split(refs, cells)
        start, wait = fetcher(at_ref, arrays, buffer, sems)
        g = pl.program_id(0)
        for slot in range(slots):

            @pl.when(g == min(slot, turns - 1))
            def _():
                start(slot)

        @pl.when(g < turns)
        def _():
            parts = [
                mm(table_from(order_ref[i], first, last), in_ref[i]).astype(jnp.bfloat16)
                for i in range(group)
            ]
            put = jnp.concatenate(parts, axis=1) + part_ref[...]
            att_ref[...] = put
            whole[pl.ds(g, 1)] = put[None]

        for slot in range(slots):

            @pl.when(g == turns + slot)
            def _():
                wait(slot)
                attended = jnp.concatenate([whole[t] for t in range(turns)], axis=1)
                out_ref[...] = mm(attended, buffer[slot]).astype(jnp.bfloat16)

    flat = [cell for cells_ in cells for cell in cells_]
    turn = lambda g: jnp.minimum(g, turns - 1)
    columns = pl.BlockSpec((rows, group * width), lambda g, at: (0, turn(g)))
    return pl.pallas_call(
        kernel,
        name="unpack_project",
        grid_spec=pltpu.PrefetchScalarGridSpec(
            num_scalar_prefetch=1,
            grid=(turns + slots,),
            in_specs=[
                pl.BlockSpec((group, 1, rows), lambda g, at: (turn(g), 0, 0)),
                pl.BlockSpec((group, last - first, width), lambda g, at: (turn(g), 0, 0)),
                columns,
            ]
            + [pl.BlockSpec(memory_space=pl.ANY)] * len(flat),
            out_specs=[
                pl.BlockSpec((rows, wide), lambda g, at: (0, jnp.maximum(g - turns, 0))),
                columns,
            ],
            scratch_shapes=[pltpu.VMEM((turns, rows, group * width), jnp.bfloat16)]
            + fetch_scratch(2 * slots, cells),
        ),
        out_shape=[
            jax.ShapeDtypeStruct((rows, slots * wide), jnp.bfloat16),
            jax.ShapeDtypeStruct((rows, heads * width), jnp.bfloat16),
        ],
    )(places, order, returned, partial, *flat)


def gather_weights(w_out):
    count = lax.axis_size("seq")
    line = count // 4
    me = lax.axis_index("seq")
    moves = {f"right{n}": [(i, i + 4) for i in range(4 * (n - 1), count - 4)] for n in range(1, line)}
    moves |= {f"left{n}": [(i + 4, i) for i in range(count - 4 * n)] for n in range(1, line)}
    moves |= {
        "x": [(i, i ^ 1) for i in range(count)],
        "y": [(i, i ^ 2) for i in range(count)],
    }

    def moved(cells, way):
        return lax.ppermute(cells, "seq", moves[way])

    half = w_out.shape[0] // 2
    own = (w_out[None, :half], w_out[None, half:])
    from_left, from_right = [w_out], [w_out]
    from_left.append(moved(w_out, "right1"))
    from_right.append(moved(w_out, "left1"))
    ways = (("y", "x"), ("x", "y"))

    def spread(cells):
        both = []
        for color, (inner, outer) in enumerate(ways):
            here = cells[color]
            over_inner = moved(here, inner)
            over_outer = moved(here, outer)
            both.append([here, over_inner, over_outer, moved(over_inner, outer)])
        return both

    near = spread(own)
    for hop in range(2, line):
        from_left.append(moved(from_left[-1], f"right{hop}"))
        from_right.append(moved(from_right[-1], f"left{hop}"))
    middle = from_left[2] + from_right[2]
    middle = [middle[None, :half], middle[None, half:]]
    mid = spread(middle)
    ends = [from_left[1] + from_right[3], from_left[3] + from_right[1]]
    ends = [jnp.stack([cell[at : at + half] for cell in ends]) for at in (0, half)]
    far = spread(ends)
    cells = [[*near[c], *mid[c], *far[c]] for c in range(2)]
    names = jnp.arange(count, dtype=jnp.int32)
    step = jnp.mod(me // 4 - names // 4, line)
    odd = step & 1
    group = jnp.where(step == 0, 0, 1 + odd)
    differ = jnp.bitwise_xor(me, names)
    x_bit, y_bit = differ & 1, (differ >> 1) & 1
    spot = jnp.where(odd == 1, step >> 1, 0)
    places = []
    for inner, outer in ((y_bit, x_bit), (x_bit, y_bit)):
        places += [4 * group + 2 * outer + inner, spot]
    return cells, jnp.stack(places)


def head_shards(queries, keys, values, route, members, pattern, w_out):
    heads, rows = route.shape
    count = lax.axis_size("seq")
    per = rows // count
    entries = pattern.shape[1] * pattern.shape[2]
    early = count // 2 + 1
    cut, cut_back = early * per, (early - 1) * per
    pattern = jnp.pad(pattern.reshape(heads, entries), ((0, 0), (0, LANES - entries)))

    def exchange(cells):
        return lax.all_to_all(cells, "seq", split_axis=0, concat_axis=0, tiled=True)

    cells, place = gather_weights(w_out)
    packed, order = pack(route, pattern, queries, keys, values, 0, cut)
    packed_rest = pack(route, pattern, queries, keys, values, cut, rows, order)
    arrived = exchange(packed)
    arrived_rest = exchange(packed_rest)
    slots, pattern = tail_of(arrived, rows, entries)
    context, kept = attend(slots, pattern, arrived, early)
    returned = exchange(context)
    context_rest, _ = attend(slots, pattern, arrived_rest, count - early, kept)
    returned_rest = exchange(context_rest)
    attended = unpack(order, returned, 0, cut_back)
    mine = lax.axis_index("tp")
    part = count // 2

    def places(which):
        return lax.dynamic_slice_in_dim(place, which * part, part, 1)

    send, attended = unpack_project(
        order, returned_rest, cut_back, rows, attended, places(1 - mine), cells
    )
    received = lax.ppermute(send, "tp", [(0, 1), (1, 0)])
    keep = project(places(mine), attended, cells)
    return (keep.astype(jnp.float32) + received.astype(jnp.float32)).astype(jnp.bfloat16)


def choose(mesh):
    count, groups = mesh.shape["seq"], mesh.shape["tp"]

    def shards(queries, keys, values, route, members, pattern, w_out):
        heads, rows = route.shape
        split = heads == count and groups == 2 and count == 4 * 4
        tiles = rows == REACH * CLUSTER and queries.shape[1] == heads * LANES
        body = head_shards if split and tiles else slot_shards
        return body(queries, keys, values, route, members, pattern, w_out)

    return shards


def solution(mesh):
    placed = (
        P("seq", "tp"),
        P("seq", "tp"),
        P("seq", "tp"),
        P("tp", "seq"),
        P("tp", "seq"),
        P("tp", "seq", None),
        P("tp", "seq"),
    )
    return jax.shard_map(
        choose(mesh), mesh=mesh, in_specs=placed, out_specs=P("seq", "tp"), check_vma=False
    )
```

```python
import jax
import jax.numpy as jnp
from jax import lax
from jax.experimental import pallas as pl
from jax.experimental.pallas import tpu as pltpu
from jax.sharding import PartitionSpec as P


CLUSTER = 256
REACH = 2


def extended_2(cells, sides, width):
    for axis, dim in sides:
        count = lax.axis_size(axis)
        ends = count - 1
        head = lax.slice_in_dim(cells, 0, width, axis=dim)
        tail = lax.slice_in_dim(cells, cells.shape[dim] - width, cells.shape[dim], axis=dim)
        cells = jnp.concatenate(
            [
                lax.ppermute(tail, axis, [(i, (i + 1) % count) for i in range(ends)]),
                cells,
                lax.ppermute(head, axis, [((i + 1) % count, i) for i in range(ends)]),
            ],
            axis=dim,
        )
    return cells


def attend_head(pieces):
    query_rows, key_rows, value_rows, pattern_rows = pieces
    head_width = query_rows.shape[1]
    cluster_count = query_rows.shape[0] // CLUSTER
    window_rows = (2 * REACH + 1) * CLUSTER
    starts = jnp.arange(cluster_count) * CLUSTER
    key_window = jax.vmap(
        lambda slot_start: lax.dynamic_slice_in_dim(key_rows, slot_start, window_rows, 0)
    )(starts)
    value_window = jax.vmap(
        lambda slot_start: lax.dynamic_slice_in_dim(value_rows, slot_start, window_rows, 0)
    )(starts)
    query_blocks = query_rows.reshape(cluster_count, CLUSTER, head_width)
    scores = jnp.einsum(
        "cqd,ckd->cqk", query_blocks, key_window, preferred_element_type=jnp.float32
    ) * head_width ** (-0.5)
    allowed = jnp.repeat(pattern_rows, CLUSTER // 2, axis=1) > 0
    scores = jnp.where(allowed[:, None, :], scores, -jnp.inf)
    row_max = jnp.max(scores, axis=-1, keepdims=True)
    exponent = jnp.exp(scores - row_max)
    weights = (exponent / jnp.sum(exponent, axis=-1, keepdims=True)).astype(jnp.bfloat16)
    context = jnp.einsum(
        "cqk,ckd->cqd", weights, value_window, preferred_element_type=jnp.float32
    ).astype(jnp.bfloat16)
    return context.reshape(query_rows.shape[0], head_width)


def buffer_index(group_of, order_key, per_peer):
    same_group = group_of[:, :, None] == group_of[:, None, :]
    earlier = order_key[:, None, :] < order_key[:, :, None]
    rank = jnp.sum((same_group & earlier).astype(jnp.int32), axis=2)
    return group_of * per_peer + rank


def slot_shards(queries, keys, values, route, members, pattern, w_out):
    rows_here = queries.shape[0]
    head_count = route.shape[0]
    head_width = queries.shape[1] // head_count
    peer_count = lax.axis_size("seq")
    per_peer = rows_here // peer_count
    local_iota = jnp.arange(rows_here, dtype=jnp.int32)
    send_index = buffer_index(route // rows_here, route, per_peer)
    local_slots = jnp.broadcast_to(local_iota[None, :], members.shape)
    arrival_index = buffer_index(members // rows_here, local_slots, per_peer)
    send_table = (send_index[:, None, :] == local_iota[None, :, None]).astype(jnp.bfloat16)
    land_table = (arrival_index[:, :, None] == local_iota[None, None, :]).astype(jnp.bfloat16)
    stacked = jnp.concatenate(
        [
            queries.reshape(rows_here, head_count, head_width),
            keys.reshape(rows_here, head_count, head_width),
            values.reshape(rows_here, head_count, head_width),
        ],
        axis=2,
    )
    packed = jnp.einsum(
        "hap,phd->had", send_table, stacked, preferred_element_type=jnp.float32
    ).astype(jnp.bfloat16)

    def outgoing(column_index):
        part_rows = packed[:, :, column_index * head_width : (column_index + 1) * head_width]
        return part_rows.reshape(head_count, peer_count, per_peer, head_width)

    sent_query, sent_key, sent_value = (
        lax.all_to_all(outgoing(0), "seq", split_axis=1, concat_axis=1, tiled=True),
        lax.all_to_all(outgoing(1), "seq", split_axis=1, concat_axis=1, tiled=True),
        lax.all_to_all(outgoing(2), "seq", split_axis=1, concat_axis=1, tiled=True),
    )
    arrived = jnp.concatenate(
        [
            sent_query.reshape(head_count, rows_here, head_width),
            sent_key.reshape(head_count, rows_here, head_width),
            sent_value.reshape(head_count, rows_here, head_width),
        ],
        axis=2,
    )
    placed = jnp.einsum(
        "hsa,had->hsd", land_table, arrived, preferred_element_type=jnp.float32
    ).astype(jnp.bfloat16)
    ordered_query = placed[:, :, :head_width]
    keys_values = jnp.stack(
        [placed[:, :, head_width : 2 * head_width], placed[:, :, 2 * head_width :]]
    )
    extended = extended_2(keys_values, (("seq", 2),), REACH * CLUSTER)
    context = lax.map(attend_head, (ordered_query, extended[0], extended[1], pattern))
    returning = jnp.einsum(
        "hsa,hsd->had", land_table, context, preferred_element_type=jnp.float32
    ).astype(jnp.bfloat16)
    returning = returning.reshape(head_count, peer_count, per_peer, head_width)
    returned = lax.all_to_all(returning, "seq", split_axis=1, concat_axis=1, tiled=True).reshape(
        head_count, rows_here, head_width
    )
    attended = jnp.einsum(
        "hap,had->phd", send_table, returned, preferred_element_type=jnp.float32
    ).astype(jnp.bfloat16)
    attended = attended.reshape(rows_here, head_count * head_width)
    partial_value = jnp.dot(
        attended,
        lax.all_gather(w_out, "seq", axis=1, tiled=True),
        preferred_element_type=jnp.float32,
    )
    mixed_out = lax.psum_scatter(
        partial_value.astype(jnp.bfloat16), "tp", scatter_dimension=1, tiled=True
    )
    return mixed_out


LANES = 128
DIGIT = 4
TAIL = 16
BLOCK = 128


def order_of(key_row):
    n = key_row.shape[1]
    key_col = jnp.broadcast_to(key_row, (LANES, n)).T
    counts = []
    for j in range(n // LANES):
        less = key_col < key_row[:, j * LANES : (j + 1) * LANES]
        counts.append(jnp.sum(jnp.where(less, 1, 0), axis=0, keepdims=True))
    return jnp.concatenate(counts, axis=1)


def table_to(order_row, first, last):
    n = order_row.shape[1]
    rows = lax.broadcasted_iota(jnp.int32, (last - first, n), 0) + first
    return jnp.where(rows == order_row, 1.0, 0.0).astype(jnp.bfloat16)


def table_from(order_row, first, last):
    n = order_row.shape[1]
    order_col = jnp.broadcast_to(order_row, (LANES, n)).T
    parts = []
    for start in range(first, last, LANES):
        lane = lax.broadcasted_iota(jnp.int32, (n, min(LANES, last - start)), 1) + start
        parts.append(jnp.where(order_col[:, : lane.shape[1]] == lane, 1.0, 0.0).astype(jnp.bfloat16))
    return jnp.concatenate(parts, axis=1) if len(parts) > 1 else parts[0]


def mm(a, b):
    return jnp.dot(a, b, preferred_element_type=jnp.float32)


def pack(route, pattern, queries, keys, values, first, last, order=None):
    heads, rows = route.shape
    width = queries.shape[1] // heads
    lines = rows // LANES
    leads = order is None
    part = last - first
    group = 2

    def emit(i, order_row, refs, out_ref):
        stacked = jnp.concatenate([ref[:, i * width : (i + 1) * width] for ref in refs], axis=1)
        put = mm(table_to(order_row, first, last), stacked).astype(jnp.bfloat16)
        for n in range(3):
            out_ref[i, n * part : (n + 1) * part] = put[:, n * width : (n + 1) * width]

    def lead(route_ref, pat_ref, q_ref, k_ref, v_ref, out_ref, order_ref):
        for i in range(group):
            h = pl.program_id(0) * group + i
            row = route_ref[pl.ds(h, 1), :]
            order_row = order_of(row)
            order_ref[i] = order_row
            emit(i, order_row, (q_ref, k_ref, v_ref), out_ref)
            slot = jnp.bitwise_and(row, rows - 1)
            high = lax.shift_right_logical(slot, DIGIT)
            low = jnp.bitwise_and(slot, (1 << DIGIT) - 1)
            at = lax.broadcasted_iota(jnp.int32, (8, rows), 0)
            digits = jnp.where(at == 0, high, jnp.where(at == 1, low, 0))
            digits = digits.astype(jnp.float32).astype(jnp.bfloat16)
            sorted_digits = lax.dot_general(
                digits,
                table_to(order_row, 0, rows),
                (((1,), (1,)), ((), ())),
                preferred_element_type=jnp.float32,
            )
            parts = [
                sorted_digits[d : d + 1, j * LANES : (j + 1) * LANES]
                for d in range(2)
                for j in range(lines)
            ]
            parts.append(pat_ref[pl.ds(h, 1), :].astype(jnp.float32))
            parts.append(jnp.zeros((TAIL - 2 * lines - 1, LANES), jnp.float32))
            out_ref[i, 3 * part :] = jnp.concatenate(parts, axis=0).astype(jnp.bfloat16)

    def follow(order_ref, q_ref, k_ref, v_ref, out_ref):
        for i in range(group):
            emit(i, order_ref[i], (q_ref, k_ref, v_ref), out_ref)

    columns = pl.BlockSpec((rows, group * width), lambda h: (0, h))
    order_spec = pl.BlockSpec((group, 1, rows), lambda h: (h, 0, 0))
    total = 3 * part + (TAIL if leads else 0)
    out_spec = pl.BlockSpec((group, total, width), lambda h: (h, 0, 0))
    out_shape = jax.ShapeDtypeStruct((heads, total, width), jnp.bfloat16)
    if not leads:
        return pl.pallas_call(
            follow,
            name="pack_rest",
            grid=(heads // group,),
            in_specs=[order_spec, columns, columns, columns],
            out_specs=out_spec,
            out_shape=out_shape,
        )(order, queries, keys, values)
    return pl.pallas_call(
        lead,
        name="pack",
        grid=(heads // group,),
        in_specs=[
            pl.BlockSpec((heads, rows), lambda h: (0, 0)),
            pl.BlockSpec((heads, LANES), lambda h: (0, 0)),
            columns,
            columns,
            columns,
        ],
        out_specs=[out_spec, order_spec],
        out_shape=[out_shape, jax.ShapeDtypeStruct((heads, 1, rows), jnp.int32)],
    )(route, pattern, queries, keys, values)


def tail_of(arrived, rows, entries):
    senders = arrived.shape[0]
    lines = rows // LANES
    tail = arrived[:, -TAIL:].astype(jnp.int32)
    slot = (tail[:, :lines] << DIGIT) + tail[:, lines : 2 * lines]
    slot = slot.reshape(senders, senders, rows // senders).transpose(1, 0, 2)
    return slot.reshape(senders, rows), tail[:, 2 * lines, :entries].reshape(-1)


def attend(slots, pattern, arrived, count, kept=None):
    nb, rows = slots.shape
    senders, _, width = arrived.shape
    per = rows // senders
    per_block = rows // CLUSTER
    window = (2 * REACH + 1) * CLUSTER
    blocks = window // BLOCK
    leads = kept is None
    lowest = 0 if leads else nb - count
    steps = count if leads else count + 1
    done = count - 1 if leads else count + 1
    ahead = rows if leads else 2 * rows
    total = (count + (1 if leads else 3)) * rows
    scale = width ** (-0.5) * 1.4426950408889634

    def kernel(pat_ref, slot_ref, q_ref, k_ref, v_ref, *refs):
        if leads:
            out_ref, q_keep, k_keep, v_keep, kbuf, vbuf, qbuf = refs
        else:
            q_kept, k_kept, v_kept, out_ref, kbuf, vbuf, qbuf = refs
        g = pl.program_id(0)

        @pl.when(g == 0)
        def _():
            zero = jnp.zeros((rows, width), jnp.bfloat16)
            vbuf[:, width:] = jnp.ones((total, width), jnp.bfloat16)
            if leads:
                kbuf[:rows, :] = zero
                vbuf[:rows, :width] = zero
            else:
                kbuf[: 2 * rows, :] = k_kept[...]
                vbuf[: 2 * rows, :width] = v_kept[...]
                qbuf[(lowest - 1) % 2] = q_kept[...]
                kbuf[total - rows :, :] = zero
                vbuf[total - rows :, :width] = zero

        @pl.when(g < count)
        def _():
            block = g + lowest
            table = table_to(slot_ref[pl.ds(block, 1), :], 0, rows)
            at = pl.multiple_of(g * rows + ahead, rows)
            put = [
                mm(table, ref[...].reshape(rows, width)).astype(jnp.bfloat16)
                for ref in (q_ref, k_ref, v_ref)
            ]
            qbuf[pl.ds(block % 2, 1)] = put[0][None]
            kbuf[pl.ds(at, rows), :] = put[1]
            vbuf[pl.ds(at, rows), :width] = put[2]
            if leads:

                @pl.when(g == count - 1)
                def _():
                    q_keep[...] = put[0]
                    k_keep[:rows, :] = kbuf[total - 2 * rows : total - rows, :]
                    v_keep[:rows, :] = vbuf[total - 2 * rows : total - rows, :width]
                    k_keep[rows:, :] = put[1]
                    v_keep[rows:, :] = put[2]

        @pl.when(g + lowest > 0)
        def _():
            b = g + lowest - 1
            base = (g - 1 if leads else g) * rows
            contexts = []
            for i in range(per_block):
                q = qbuf[pl.ds(b % 2, 1), i * CLUSTER : (i + 1) * CLUSTER, :][0]
                at = pl.multiple_of(base + i * CLUSTER, CLUSTER)
                scores = lax.dot_general(
                    q,
                    kbuf[pl.ds(at, window), :],
                    (((1,), (1,)), ((), ())),
                    preferred_element_type=jnp.float32,
                )
                parts = []
                for j in range(blocks):
                    allowed = pat_ref[(b * per_block + i) * blocks + j] > 0
                    shift = jnp.where(allowed, 0.0, -jnp.inf)
                    parts.append(scores[:, j * BLOCK : (j + 1) * BLOCK] + shift)
                most = parts[0]
                for part in parts[1:]:
                    most = jnp.maximum(most, part)
                most = jnp.max(most, axis=1, keepdims=True)
                weights = jnp.concatenate(
                    [jnp.exp2((part - most) * scale).astype(jnp.bfloat16) for part in parts], axis=1
                )
                both = mm(weights, vbuf[pl.ds(at, window), :])
                contexts.append((both[:, :width] / both[:, width:]).astype(jnp.bfloat16))
            context = jnp.concatenate(contexts, axis=0)
            back = mm(table_from(slot_ref[pl.ds(b, 1), :], 0, rows), context).astype(jnp.bfloat16)
            out_ref[...] = back.reshape(senders, per, width)

    whole = lambda *shape: pl.BlockSpec(shape, lambda g, p: (0,) * len(shape))
    incoming = [
        pl.BlockSpec(
            (senders, per, width), lambda g, p, i=i: (0, i * count + jnp.minimum(g, count - 1), 0)
        )
        for i in range(3)
    ]
    keep_specs = [whole(rows, width), whole(2 * rows, width), whole(2 * rows, width)]
    out_specs = [
        pl.BlockSpec(
            (senders, per, width), lambda g, p: (0, jnp.maximum(g - 1, 0) if leads else g, 0)
        )
    ]
    out_shape = [jax.ShapeDtypeStruct((senders, done * per, width), jnp.bfloat16)]
    if leads:
        out_specs += keep_specs
        out_shape += [
            jax.ShapeDtypeStruct((n * rows, width), jnp.bfloat16) for n in (1, 2, 2)
        ]
    out = pl.pallas_call(
        kernel,
        name="attend" if leads else "attend_rest",
        grid_spec=pltpu.PrefetchScalarGridSpec(
            num_scalar_prefetch=1,
            grid=(steps,),
            in_specs=[whole(nb, rows), *incoming] + ([] if leads else keep_specs),
            out_specs=out_specs,
            scratch_shapes=[
                pltpu.VMEM((total, width), jnp.bfloat16),
                pltpu.VMEM((total, 2 * width), jnp.bfloat16),
                pltpu.VMEM((2, rows, width), jnp.bfloat16),
            ],
        ),
        out_shape=out_shape,
    )(pattern, slots, arrived, arrived, arrived, *(() if leads else kept))
    return out[0], out[1:]


def unpack(order, returned, first, last):
    heads, _, width = returned.shape
    rows = order.shape[2]
    group = 4

    def kernel(order_ref, in_ref, out_ref):
        parts = [
            mm(table_from(order_ref[i], first, last), in_ref[i]).astype(jnp.bfloat16)
            for i in range(group)
        ]
        out_ref[...] = jnp.concatenate(parts, axis=1)

    return pl.pallas_call(
        kernel,
        name="unpack",
        grid=(heads // group,),
        in_specs=[
            pl.BlockSpec((group, 1, rows), lambda h: (h, 0, 0)),
            pl.BlockSpec((group, last - first, width), lambda h: (h, 0, 0)),
        ],
        out_specs=pl.BlockSpec((rows, group * width), lambda h: (0, h)),
        out_shape=jax.ShapeDtypeStruct((rows, heads * width), jnp.bfloat16),
    )(order, returned)


def fetcher(at_ref, arrays, buffer, sems):
    half, cols = arrays[0][0].shape[1:]

    def copy(p, c, source):
        to = buffer.at[p // 2, pl.ds(c * half, half), pl.ds(p % 2 * cols, cols)]
        return pltpu.make_async_copy(source, to, sems.at[p, c])

    def start(slot):
        for p in (2 * slot, 2 * slot + 1):
            for c, kinds in enumerate(arrays):
                for kind, array in enumerate(kinds):

                    @pl.when(at_ref[2 * c, p] == kind)
                    def _():
                        copy(p, c, array.at[at_ref[2 * c + 1, p]]).start()

    def wait(slot):
        for p in (2 * slot, 2 * slot + 1):
            for c, kinds in enumerate(arrays):
                copy(p, c, kinds[0].at[0]).wait()

    return start, wait


def fetch_scratch(count, cells):
    half, cols = cells[0][0].shape[1:]
    return [
        pltpu.VMEM((count // 2, len(cells) * half, 2 * cols), jnp.bfloat16),
        pltpu.SemaphoreType.DMA((count, len(cells))),
    ]


def split(refs, cells):
    kinds = len(cells[0])
    return [refs[c * kinds : (c + 1) * kinds] for c in range(len(cells))], refs[len(cells) * kinds :]


def project(places, attended, cells):
    slots = places.shape[1] // 2
    rows, depth = attended.shape
    wide = 2 * cells[0][0].shape[2]

    def kernel(at_ref, a_ref, *refs):
        arrays, (out_ref, buffer, sems) = split(refs, cells)
        start, wait = fetcher(at_ref, arrays, buffer, sems)
        j = pl.program_id(0)
        for slot in range(slots):

            @pl.when(j == max(slot - 2, 0))
            def _():
                start(slot)

        for slot in range(slots):

            @pl.when(j == slot)
            def _():
                wait(slot)

        at = pl.ds(pl.multiple_of(j * wide, wide), wide)
        out_ref[:, at] = mm(a_ref[...], buffer[pl.ds(j, 1)][0]).astype(jnp.bfloat16)

    flat = [cell for group in cells for cell in group]
    return pl.pallas_call(
        kernel,
        name="project",
        grid_spec=pltpu.PrefetchScalarGridSpec(
            num_scalar_prefetch=1,
            grid=(slots,),
            in_specs=[pl.BlockSpec((rows, depth), lambda j, at: (0, 0))]
            + [pl.BlockSpec(memory_space=pl.ANY)] * len(flat),
            out_specs=pl.BlockSpec(memory_space=pltpu.VMEM),
            scratch_shapes=fetch_scratch(2 * slots, cells),
        ),
        out_shape=pltpu.VMEM((rows, slots * wide), jnp.bfloat16),
    )(places, attended, *flat)


def unpack_project(order, returned, first, last, partial, places, cells):
    heads, _, width = returned.shape
    rows = order.shape[2]
    slots = places.shape[1] // 2
    wide = 2 * cells[0][0].shape[2]
    group = 4
    turns = heads // group

    def kernel(at_ref, order_ref, in_ref, part_ref, *refs):
        arrays, (out_ref, att_ref, whole, buffer, sems) = split(refs, cells)
        start, wait = fetcher(at_ref, arrays, buffer, sems)
        g = pl.program_id(0)
        for slot in range(slots):

            @pl.when(g == min(slot, turns - 1))
            def _():
                start(slot)

        @pl.when(g < turns)
        def _():
            parts = [
                mm(table_from(order_ref[i], first, last), in_ref[i]).astype(jnp.bfloat16)
                for i in range(group)
            ]
            put = jnp.concatenate(parts, axis=1) + part_ref[...]
            att_ref[...] = put
            whole[pl.ds(g, 1)] = put[None]

        for slot in range(slots):

            @pl.when(g == turns + slot)
            def _():
                wait(slot)
                attended = jnp.concatenate([whole[t] for t in range(turns)], axis=1)
                out_ref[...] = mm(attended, buffer[slot]).astype(jnp.bfloat16)

    flat = [cell for cells_ in cells for cell in cells_]
    turn = lambda g: jnp.minimum(g, turns - 1)
    columns = pl.BlockSpec((rows, group * width), lambda g, at: (0, turn(g)))
    return pl.pallas_call(
        kernel,
        name="unpack_project",
        grid_spec=pltpu.PrefetchScalarGridSpec(
            num_scalar_prefetch=1,
            grid=(turns + slots,),
            in_specs=[
                pl.BlockSpec((group, 1, rows), lambda g, at: (turn(g), 0, 0)),
                pl.BlockSpec((group, last - first, width), lambda g, at: (turn(g), 0, 0)),
                columns,
            ]
            + [pl.BlockSpec(memory_space=pl.ANY)] * len(flat),
            out_specs=[
                pl.BlockSpec((rows, wide), lambda g, at: (0, jnp.maximum(g - turns, 0))),
                columns,
            ],
            scratch_shapes=[pltpu.VMEM((turns, rows, group * width), jnp.bfloat16)]
            + fetch_scratch(2 * slots, cells),
        ),
        out_shape=[
            jax.ShapeDtypeStruct((rows, slots * wide), jnp.bfloat16),
            jax.ShapeDtypeStruct((rows, heads * width), jnp.bfloat16),
        ],
    )(places, order, returned, partial, *flat)


def gather_weights(w_out):
    count = lax.axis_size("seq")
    line = count // 4
    me = lax.axis_index("seq")
    moves = {f"right{n}": [(i, i + 4) for i in range(4 * (n - 1), count - 4)] for n in range(1, line)}
    moves |= {f"left{n}": [(i + 4, i) for i in range(count - 4 * n)] for n in range(1, line)}
    moves |= {
        "x": [(i, i ^ 1) for i in range(count)],
        "y": [(i, i ^ 2) for i in range(count)],
    }

    def moved(cells, way):
        return lax.ppermute(cells, "seq", moves[way])

    half = w_out.shape[0] // 2
    own = (w_out[None, :half], w_out[None, half:])
    from_left, from_right = [w_out], [w_out]
    from_left.append(moved(w_out, "right1"))
    from_right.append(moved(w_out, "left1"))
    ways = (("y", "x"), ("x", "y"))

    def spread(cells):
        both = []
        for color, (inner, outer) in enumerate(ways):
            here = cells[color]
            over_inner = moved(here, inner)
            over_outer = moved(here, outer)
            both.append([here, over_inner, over_outer, moved(over_inner, outer)])
        return both

    near = spread(own)
    for hop in range(2, line):
        from_left.append(moved(from_left[-1], f"right{hop}"))
        from_right.append(moved(from_right[-1], f"left{hop}"))
    middle = from_left[2] + from_right[2]
    middle = [middle[None, :half], middle[None, half:]]
    mid = spread(middle)
    ends = [from_left[1] + from_right[3], from_left[3] + from_right[1]]
    ends = [jnp.stack([cell[at : at + half] for cell in ends]) for at in (0, half)]
    far = spread(ends)
    cells = [[*near[c], *mid[c], *far[c]] for c in range(2)]
    names = jnp.arange(count, dtype=jnp.int32)
    step = jnp.mod(me // 4 - names // 4, line)
    odd = step & 1
    group = jnp.where(step == 0, 0, 1 + odd)
    differ = jnp.bitwise_xor(me, names)
    x_bit, y_bit = differ & 1, (differ >> 1) & 1
    spot = jnp.where(odd == 1, step >> 1, 0)
    places = []
    for inner, outer in ((y_bit, x_bit), (x_bit, y_bit)):
        places += [4 * group + 2 * outer + inner, spot]
    return cells, jnp.stack(places)


def head_shards(queries, keys, values, route, members, pattern, w_out):
    heads, rows = route.shape
    count = lax.axis_size("seq")
    per = rows // count
    entries = pattern.shape[1] * pattern.shape[2]
    early = count // 2 + 2
    cut, cut_back = early * per, (early - 1) * per
    pattern = jnp.pad(pattern.reshape(heads, entries), ((0, 0), (0, LANES - entries)))

    def exchange(cells):
        return lax.all_to_all(cells, "seq", split_axis=0, concat_axis=0, tiled=True)

    cells, place = gather_weights(w_out)
    packed, order = pack(route, pattern, queries, keys, values, 0, cut)
    packed_rest = pack(route, pattern, queries, keys, values, cut, rows, order)
    arrived = exchange(packed)
    arrived_rest = exchange(packed_rest)
    slots, pattern = tail_of(arrived, rows, entries)
    context, kept = attend(slots, pattern, arrived, early)
    returned = exchange(context)
    context_rest, _ = attend(slots, pattern, arrived_rest, count - early, kept)
    returned_rest = exchange(context_rest)
    attended = unpack(order, returned, 0, cut_back)
    mine = lax.axis_index("tp")
    part = count // 2

    def places(which):
        return lax.dynamic_slice_in_dim(place, which * part, part, 1)

    send, attended = unpack_project(
        order, returned_rest, cut_back, rows, attended, places(1 - mine), cells
    )
    received = lax.ppermute(send, "tp", [(0, 1), (1, 0)])
    keep = project(places(mine), attended, cells)
    return (keep.astype(jnp.float32) + received.astype(jnp.float32)).astype(jnp.bfloat16)


def choose(mesh):
    count, groups = mesh.shape["seq"], mesh.shape["tp"]

    def shards(queries, keys, values, route, members, pattern, w_out):
        heads, rows = route.shape
        split = heads == count and groups == 2 and count == 4 * 4
        tiles = rows == REACH * CLUSTER and queries.shape[1] == heads * LANES
        body = head_shards if split and tiles else slot_shards
        return body(queries, keys, values, route, members, pattern, w_out)

    return shards


def solution(mesh):
    placed = (
        P("seq", "tp"),
        P("seq", "tp"),
        P("seq", "tp"),
        P("tp", "seq"),
        P("tp", "seq"),
        P("tp", "seq", None),
        P("tp", "seq"),
    )
    return jax.shard_map(
        choose(mesh), mesh=mesh, in_specs=placed, out_specs=P("seq", "tp"), check_vma=False
    )
```
